256 devices in a mesh: gx: 4 (over y), yz: 64 (over z, x, core).
Axes of the slice: x: 4, y: 4, z: 8, core: 2. Of those that a mesh axis runs over, the one named last changes fastest.
Arguments:
- spin_vectors: float32 [3, 2, 16, 128, 128], P(None, None, 'gx', 'yz'), may hold values from -1 to 1, as said below
- pair_weight: float32 [112, 128], replicated, may hold values from -0.5 to 0.5
- mix_weight: float32 [128, 128], replicated, may hold values from -0.5 to 0.5
- mix_bias: float32 [128], replicated, may hold values from -3 to 3
- out_weight: float32 [128], replicated, may hold values from -0.5 to 0.5
Outputs:
- spins_next: float32 [3, 2, 16, 128, 128], P(None, None, 'gx', 'yz')
- field_next: float32 [3, 2, 16, 128, 128], P(None, None, 'gx', 'yz')
The draws below stay inside these ranges and needn't reach their ends.
Inputs may be any that keep to these rules, and one draw needn't show every extreme that they name: `spin_vectors`: every atom's spin has unit length.
All inputs are finite; a program needn't handle non-finite values.
Results may differ from the reference program's by a relative error of at most 0.0003.
Values sent between devices are 32-bit elements; how exact they have to be, the bound alone decides.
A program may use at most 128 MiB of HBM per device.

```python
import math
from functools import reduce
import jax
import jax.numpy as jnp
from jax import lax

CX = 4
CY = 2
CZ = 128
NB = 8
K = 128
H = 128
NX = 16
NY = 128


def draw_spin_vectors(key, part):
    raw_draw = jax.random.normal(jax.random.fold_in(key, 11), (3, 2, NX, NY, CZ), jnp.float32)
    length = jnp.sqrt(jnp.sum(raw_draw * raw_draw, axis=0, keepdims=True))
    return raw_draw / jnp.maximum(length, 1e-06)


def centred(rng, shape, spread, limit, kind=jnp.bfloat16):
    values = spread * jax.random.normal(rng, shape, jnp.float32)
    return jnp.clip(values, min=-limit, max=limit).astype(kind)


def setup_inputs(seed: int = 0) -> dict:
    seeds = jax.random.split(jax.random.key(seed), 6)
    return {
        "spin_vectors": draw_spin_vectors(jax.random.fold_in(seeds[5], 71), 0),
        "pair_weight": centred(seeds[1], (14 * NB, K), (14 * NB) ** -0.5, 0.5, jnp.float32),
        "mix_weight": centred(seeds[2], (K, H), K ** -0.5, 0.5, jnp.float32),
        "mix_bias": centred(seeds[3], (H,), 0.5, 3.0, jnp.float32),
        "out_weight": centred(seeds[4], (H,), H ** -0.5, 0.5, jnp.float32),
    }


time_step = 0.1
first_shell = [(-1, -1, -1), (-1, -1, 0), (-1, 0, -1), (-1, 0, 0), (0, -1, -1), (0, -1, 0), (0, 0, -1), (0, 0, 0)]
second_shell = [(1, 0, 0), (-1, 0, 0), (0, 1, 0), (0, -1, 0), (0, 0, 1), (0, 0, -1)]

def bond_list(lattice):
    result = []
    for step_x, step_y, step_z in first_shell:
        if lattice == 0:
            result.append((1, step_x, step_y, step_z))
        else:
            result.append((0, -step_x, -step_y, -step_z))
    for step_x, step_y, step_z in second_shell:
        result.append((lattice, step_x, step_y, step_z))
    return result

def partner(bond_index):
    if bond_index < 8:
        return bond_index
    return 8 + (bond_index - 8 ^ 1)

def shifted(padded, target, step_x, step_y, step_z, width_x, width_y):
    window = padded[:, target, 1 + step_x:1 + step_x + width_x, 1 + step_y:1 + step_y + width_y, :]
    return jnp.roll(window, -step_z, axis=-1)

def coefficients(centre, padded, pair_weight, mix_weight, mix_bias, out_weight):
    width_x, width_y, width_z = (centre.shape[2], centre.shape[3], centre.shape[4])
    cosines = []
    for lattice in range(2):
        column = []
        for bond_entry in bond_list(lattice):
            target, step_x, step_y, step_z = bond_entry
            neighbour = shifted(padded, target, step_x, step_y, step_z, width_x, width_y)
            column.append(lax.optimization_barrier(jnp.sum(centre[:, lattice] * neighbour, axis=0)))
        cosines.append(jnp.stack(column, 0))
    cosine = jnp.stack(cosines, 1)
    first_kind = [jnp.ones_like(cosine), cosine]
    second_kind = [jnp.ones_like(cosine), 2.0 * cosine]
    for degree in range(2, NB + 1):
        first_kind.append(2.0 * cosine * first_kind[-1] - first_kind[-2])
        second_kind.append(2.0 * cosine * second_kind[-1] - second_kind[-2])
    atom_count = 2 * width_x * width_y * width_z
    features = jnp.stack(first_kind[1:NB + 1], 1).reshape(14 * NB, atom_count)
    slopes = jnp.stack([(degree + 1) * second_kind[degree] for degree in range(NB)], 1).reshape(14, NB, atom_count)
    contract_lead = (((0,), (0,)), ((), ()))
    best = lax.Precision.HIGHEST
    basis_vals = lax.dot_general(pair_weight, features, contract_lead, precision=best, preferred_element_type=jnp.float32)
    hidden = jnp.tanh(lax.dot_general(mix_weight, basis_vals, contract_lead, precision=best, preferred_element_type=jnp.float32) + mix_bias[:, None])
    hidden_grad = out_weight[:, None] * (1.0 - hidden * hidden)
    basis_grad = jnp.dot(mix_weight, hidden_grad, precision=best, preferred_element_type=jnp.float32)
    feature_grad = jnp.dot(pair_weight, basis_grad, precision=best, preferred_element_type=jnp.float32).reshape(14, NB, atom_count)
    return lax.optimization_barrier(jnp.sum(feature_grad * slopes, axis=1)).reshape(14, 2, width_x, width_y, width_z)

def field_from(coeff_own, coeff_padded, spins_padded):
    width_x, width_y = (coeff_own.shape[2], coeff_own.shape[3])
    fields = []
    for lattice in range(2):
        term_list = []
        for bond_index, bond_entry in enumerate(bond_list(lattice)):
            target, step_x, step_y, step_z = bond_entry
            mate = partner(bond_index)
            partner_coeff = shifted(coeff_padded[mate:mate + 1], target, step_x, step_y, step_z, width_x, width_y)[0]
            neighbour = shifted(spins_padded, target, step_x, step_y, step_z, width_x, width_y)
            term_list.append((coeff_own[bond_index, lattice] + partner_coeff) * neighbour)
        fields.append(-reduce(jnp.add, term_list))
    return jnp.stack(fields, 1)

def rotate(spin_now, field_now):
    angle_vec = time_step * field_now
    angle_size = jnp.sqrt(lax.optimization_barrier(jnp.sum(angle_vec * angle_vec, axis=0)))
    cross_term = jnp.cross(angle_vec, spin_now, axis=0)
    projection = lax.optimization_barrier(jnp.sum(angle_vec * spin_now, axis=0))
    half_sinc = jnp.sinc(angle_size / (2.0 * math.pi))
    return jnp.cos(angle_size) * spin_now + jnp.sinc(angle_size / math.pi) * cross_term + 0.5 * half_sinc * half_sinc * projection * angle_vec

def sectors(size_x, size_y, size_z):
    shape = (size_x, size_y, size_z)
    along_x = (lax.broadcasted_iota(jnp.int32, shape, 0) % CX >= CX // 2).astype(jnp.int32)
    along_y = (lax.broadcasted_iota(jnp.int32, shape, 1) % CY >= CY // 2).astype(jnp.int32)
    along_z = (lax.broadcasted_iota(jnp.int32, shape, 2) % CZ >= CZ // 2).astype(jnp.int32)
    return 4 * along_x + 2 * along_y + along_z

def evaluate(spin_now, pair_weight, mix_weight, mix_bias, out_weight):
    padded = jnp.pad(spin_now, ((0, 0), (0, 0), (1, 1), (1, 1), (0, 0)), mode='wrap')

    def plane_coeff(position):
        slab_block = lax.dynamic_slice_in_dim(padded, position, 3, 2)
        return coefficients(slab_block[:, :, 1:2, 1:-1], slab_block, pair_weight, mix_weight, mix_bias, out_weight)
    planes = lax.map(plane_coeff, jnp.arange(NX, dtype=jnp.int32))
    coeff_all = jnp.moveaxis(planes[:, :, :, 0], 0, 2)
    coeff_padded = jnp.pad(coeff_all, ((0, 0), (0, 0), (1, 1), (1, 1), (0, 0)), mode='wrap')
    return field_from(coeff_all, coeff_padded, padded)

def reference(spin_vectors, pair_weight, mix_weight, mix_bias, out_weight):
    sector = sectors(NX, NY, CZ)
    spin_now = spin_vectors
    for colour in range(8):
        field_now = evaluate(spin_now, pair_weight, mix_weight, mix_bias, out_weight)
        spin_now = jnp.where(sector[None, None] == colour, rotate(spin_now, field_now), spin_now)
    return (spin_now, evaluate(spin_now, pair_weight, mix_weight, mix_bias, out_weight))
```

```python
import functools

import jax
import jax.numpy as jnp
from jax import lax
from jax.experimental import pallas as pl
from jax.experimental.pallas import tpu as pltpu
from jax.sharding import PartitionSpec as P

MESH = pl.DeviceIdType.MESH
NB = 8
NXI = 6
NT = 2 * NXI * 8
TIME_STEP = 0.1
CHUNK = 4
F32 = jnp.float32
BF16 = jnp.bfloat16

FIRST = [(i, j, k) for i in (-1, 0) for j in (-1, 0) for k in (-1, 0)]
SECOND = [(1, 0, 0), (-1, 0, 0), (0, 1, 0), (0, -1, 0), (0, 0, 1), (0, 0, -1)]
DELTAS = (1, -1, 2, -2)
GX_DELTAS = (0, 1, -1, 2, -2)


def bond_list(sub):
    sign = 1 - 2 * sub
    result = [(1 - sub, sign * i, sign * j, sign * k) for i, j, k in FIRST]
    return result + [(sub, i, j, k) for i, j, k in SECOND]


BONDS = (bond_list(0), bond_list(1))


def partner(o):
    return o if o < 8 else 8 + ((o - 8) ^ 1)


def row_shift(sub, target, dy):
    return dy + target - sub


def with_neighbours(atoms):
    result = set(atoms)
    for sub, x, y, z in atoms:
        for target, dx, dy, dz in BONDS[sub]:
            result.add((target, x + dx, y + dy, z + dz))
    return result


def columns_of(atoms):
    return sorted({atom[:3] for atom in atoms})


MAIN = columns_of(with_neighbours([(s, x, 0, 0) for s in (0, 1) for x in (0, 1)]))
LOW_SIDE = columns_of(with_neighbours([(1, x, -2, 63) for x in (0, 1)]))
HIGH_SIDE = columns_of(with_neighbours([(0, x, 2, 0) for x in (0, 1)]))
LOW_SIDE = [c for c in LOW_SIDE if c not in MAIN]
HIGH_SIDE = [c for c in HIGH_SIDE if c not in MAIN]
FINAL = columns_of(
    with_neighbours([(s, x, y, 0) for s in (0, 1) for x in range(4) for y in (0, 1)])
)


def tile(sub, xi, slot, half):
    return half * NT + (sub * NXI + xi) * 8 + slot


def column_tile(column, half):
    sub, x, y = column
    return tile(sub, x + 1, y + 3 + sub, half)


def rolled(value, dz):
    return value if dz == 0 else pltpu.roll(value, (-dz) % 128, value.ndim - 1)


def kernel(
    n_gx,
    n_yz,
    spin_ref,
    pair_ref,
    mix_ref,
    bias_ref,
    out_w_ref,
    spin_out,
    field_out,
    state,
    cosine,
    slope,
    first_w,
    second_w,
    scratch_w,
    start_yz,
    start_gx,
    send_buf,
    got_yz,
    got_gx,
    start_send,
    start_recv,
    send_sem,
    recv_yz,
    recv_gx,
):
    gx = lax.axis_index("gx")
    yz = lax.axis_index("yz")

    def device(dgx, dyz):
        return (lax.rem(gx + dgx + n_gx, n_gx), lax.rem(yz + dyz + n_yz, n_yz))

    barrier = pltpu.get_barrier_semaphore()
    partners = [(0, d) for d in DELTAS] + [(s, d) for s in (1, -1) for d in GX_DELTAS]
    for dgx, dyz in partners:
        pl.semaphore_signal(barrier, inc=1, device_id=device(dgx, dyz), device_id_type=MESH)

    scratch_w[...] = jnp.zeros((128, 128), F32)
    for k in range(NB):
        scratch_w[16 * k : 16 * k + 8, :] = pair_ref[pl.ds(k, 8, stride=8), :]
        scratch_w[16 * k + 8 : 16 * k + 14, :] = pair_ref[pl.ds(64 + k, 6, stride=8), :]
    merged = jnp.dot(
        scratch_w[...],
        mix_ref[...],
        precision=lax.Precision.HIGHEST,
        preferred_element_type=F32,
    )
    row = lax.broadcasted_iota(jnp.int32, (128, 128), 0)
    with_bias = jnp.where(row == 14, jnp.broadcast_to(bias_ref[...], (128, 128)), merged)
    degree = (row // 16 + 1).astype(F32)
    scaled = -merged * degree * jnp.broadcast_to(out_w_ref[...], (128, 128))

    def stacked(matrix):
        high = matrix.astype(BF16)
        low = (matrix - high.astype(F32)).astype(BF16)
        return jnp.concatenate(
            [jnp.concatenate([high, high], 1), jnp.concatenate([low, low], 1)], 0
        )

    first_w[...] = stacked(with_bias.T)
    second_w[...] = stacked(scaled)
    cosine[...] = jnp.ones(cosine.shape, F32)
    slope[...] = jnp.zeros(slope.shape, F32)
    state[...] = jnp.zeros(state.shape, F32)

    pl.semaphore_wait(barrier, len(partners))

    starts = []
    for j, d in enumerate(DELTAS):
        starts.append(
            pltpu.make_async_remote_copy(
                src_ref=spin_ref,
                dst_ref=start_yz.at[j],
                send_sem=start_send.at[j],
                recv_sem=start_recv.at[j],
                device_id=device(0, d),
                device_id_type=MESH,
            )
        )
    for j, d in enumerate(GX_DELTAS):
        starts.append(
            pltpu.make_async_remote_copy(
                src_ref=spin_ref.at[:, :, 2:4],
                dst_ref=start_gx.at[j],
                send_sem=start_send.at[4 + j],
                recv_sem=start_recv.at[4 + j],
                device_id=device(1, d),
                device_id_type=MESH,
            )
        )
    for copy in starts:
        copy.start()

    def put(value_of_sub, first_x, count, y, rows):
        for sub in (0, 1):
            r = y + 4 + sub
            state[1, :, sub, pl.ds(first_x, count), r : r + rows, :] = value_of_sub(sub)

    def roll_all(first_x, count):
        for sub in (0, 1):
            value = state[1, :, sub, pl.ds(first_x, count), :, :]
            state[0, :, sub, pl.ds(first_x, count), :, :] = rolled(value, -1)
            state[2, :, sub, pl.ds(first_x, count), :, :] = rolled(value, 1)

    put(lambda sub: spin_ref[:, sub], 2, 4, 0, 2)
    for copy in starts:
        copy.wait()
    for j, d in enumerate(DELTAS):
        put(lambda sub: start_yz[j, :, sub], 2, 4, -2 * d, 2)
    for j, d in enumerate(GX_DELTAS):
        put(lambda sub: start_gx[j, :, sub], 0, 2, -2 * d, 2)
    roll_all(0, 6)

    def cosines(first_x, count, y0):
        r0 = 1 + y0
        for sub in (0, 1):
            centre = state[1, :, sub, pl.ds(first_x, count), r0 : r0 + 8, :]
            for o, (target, dx, dy, dz) in enumerate(BONDS[sub]):
                r = r0 + row_shift(sub, target, dy)
                other = state[1 + dz, :, target, pl.ds(first_x + dx, count), r : r + 8, :]
                product = centre * other
                value = product[0] + product[1] + product[2]
                for xi in range(count):
                    at = tile(sub, xi, 0, o // 8) * 8 + o % 8
                    cosine[pl.ds(at, 8, stride=8), :] = value[xi]

    def load_cosine(column):
        halves = []
        for half in (0, 1):
            at = column_tile(column, half) * 8
            halves.append(cosine[at : at + 8, :])
        return jnp.concatenate(halves, 0)

    def store_slope(column, value):
        for half in (0, 1):
            at = column_tile(column, half) * 8 + 8
            slope[at : at + 8, :] = value[8 * half : 8 * half + 8, :]

    def product(weight, value):
        high = value.astype(BF16)
        low = (value - high.astype(F32)).astype(BF16)
        wide = jnp.dot(
            weight[...], jnp.concatenate([high, low], 0), preferred_element_type=F32
        )
        return wide[:128] + wide[128:]

    def network(values):
        results = []
        for begin in range(0, len(values), CHUNK):
            part = values[begin : begin + CHUNK]
            c = jnp.concatenate(part, 1)
            twice = c + c
            firsts = [jnp.ones_like(c), c]
            seconds = [jnp.ones_like(c), twice]
            for _ in range(2, NB + 1):
                firsts.append(twice * firsts[-1] - firsts[-2])
                seconds.append(twice * seconds[-1] - seconds[-2])
            u = jnp.tanh(product(first_w, jnp.concatenate(firsts[1:], 0)))
            d = product(second_w, 1.0 - u * u)
            g = d[0:16]
            for k in range(1, NB):
                g = g + d[16 * k : 16 * k + 16] * seconds[k]
            results += [g[:, 128 * j : 128 * j + 128] for j in range(len(part))]
        return results

    lane = lax.broadcasted_iota(jnp.int32, (16, 128), 1)

    def packed(groups):
        result = None
        for first, columns in groups:
            order = lax.rem(lane + (256 - first), 128)
            for m, column in enumerate(columns):
                value = load_cosine(column)
                if m:
                    value = pltpu.roll(value, 4 * m, 1)
                if result is None:
                    result = value
                else:
                    inside = (order >= 4 * m) & (order < 4 * m + 4)
                    result = jnp.where(inside, value, result)
        return result

    def packed_pair(columns):
        result = None
        low = lax.rem(lane + (256 - 63), 128)
        high = lax.rem(lane + (256 - 125), 128)
        for m, column in enumerate(columns):
            value = load_cosine(column)
            if m:
                value = pltpu.roll(value, 4 * m, 1)
                inside = ((low >= 4 * m) & (low < 4 * m + 4)) | (
                    (high >= 4 * m) & (high < 4 * m + 4)
                )
                value = jnp.where(inside, value, result)
            result = value
        return result

    def spread(value, columns):
        for m, column in enumerate(columns):
            store_slope(column, pltpu.roll(value, 128 - 4 * m, 1) if m else value)

    def fields(sub, xi0, count, first_x, y0):
        r0 = 1 + y0
        total = None
        for o, (target, dx, dy, dz) in enumerate(BONDS[sub]):
            mate = partner(o)
            shift = row_shift(sub, target, dy)
            coefficients = []
            for xi in range(xi0, xi0 + count):
                at = (tile(sub, xi, 0, o // 8) + 1) * 8 + o % 8
                own = slope[pl.ds(at, 8, stride=8), :]
                at = (tile(target, xi + dx, shift, mate // 8) + 1) * 8 + mate % 8
                theirs = slope[pl.ds(at, 8, stride=8), :]
                coefficients.append((own + rolled(theirs, dz))[None])
            coefficient = jnp.concatenate(coefficients, 0)
            spins = state[
                1 + dz,
                :,
                target,
                pl.ds(first_x + xi0 + dx, count),
                r0 + shift : r0 + shift + 8,
                :,
            ]
            term = coefficient[None] * spins
            total = term if total is None else total + term
        return total

    def rotate(spin, field):
        w = [TIME_STEP * field[c] for c in range(3)]
        s = [spin[c] for c in range(3)]
        square = w[0] * w[0] + w[1] * w[1] + w[2] * w[2]
        tiny = square < 1e-30
        size = jnp.sqrt(jnp.where(tiny, 1.0, square))
        sine, cosine_half = jnp.sin(0.5 * size), jnp.cos(0.5 * size)
        inverse = 1.0 / size
        half = jnp.where(tiny, 0.5, sine * inverse)
        ratio = 2.0 * half * jnp.where(tiny, 1.0, cosine_half)
        versine = 2.0 * half * half
        turn = 1.0 - versine * jnp.where(tiny, 0.0, square)
        along = versine * (w[0] * s[0] + w[1] * s[1] + w[2] * s[2])
        cross = [
            w[1] * s[2] - w[2] * s[1],
            w[2] * s[0] - w[0] * s[2],
            w[0] * s[1] - w[1] * s[0],
        ]
        return jnp.concatenate(
            [(turn * s[c] + ratio * cross[c] + along * w[c])[None] for c in range(3)], 0
        )

    shape = (3, 2, 8, 128)
    slot_of = lax.broadcasted_iota(jnp.int32, shape, 2)
    z_of = lax.broadcasted_iota(jnp.int32, shape, 3)
    seam = ((z_of >= 64) & (z_of < 66)) | (z_of >= 126)

    def write_targets(sub, first_x, y0, value):
        r0 = 1 + y0
        for dz in (-1, 0, 1):
            state[1 + dz, :, sub, pl.ds(first_x + 1, 2), r0 : r0 + 8, :] = rolled(value, dz)

    def phase(h, y0):
        x0 = 2 * h
        first_x = x0 + 1
        r0 = 1 + y0
        cosines(first_x, 4, y0)
        sides = packed([(62, LOW_SIDE), (126, HIGH_SIDE)])
        results = network([load_cosine(c) for c in MAIN] + [sides])
        for column, value in zip(MAIN, results):
            store_slope(column, value)
        spread(results[-1], LOW_SIDE)
        spread(results[-1], HIGH_SIDE)
        old, trial = [], []
        for sub in (0, 1):
            spin = state[1, :, sub, pl.ds(first_x + 1, 2), r0 : r0 + 8, :]
            old.append(spin)
            trial.append(rotate(spin, fields(sub, 1, 2, first_x, y0)))
        for sub in (0, 1):
            if sub == 0:
                extra = (slot_of == 5) & (z_of == 0)
            else:
                extra = (slot_of == 2) & (z_of == 63)
            change = ((slot_of == 3 + sub) & (z_of < 64)) | extra
            write_targets(sub, first_x, y0, jnp.where(change, trial[sub], old[sub]))
        cosines(first_x, 4, y0)
        groups = (MAIN[:9], MAIN[9:])
        results = network([packed_pair(columns) for columns in groups])
        for columns, value in zip(groups, results):
            spread(value, columns)
        final = []
        for sub in (0, 1):
            spin = state[1, :, sub, pl.ds(first_x + 1, 2), r0 : r0 + 8, :]
            again = rotate(spin, fields(sub, 1, 2, first_x, y0))
            late = (slot_of == 3 + sub) & (z_of >= 64)
            final.append(jnp.where(late, jnp.where(seam, again, trial[sub]), spin))
        for sub in (0, 1):
            write_targets(sub, first_x, y0, final[sub])
            send_buf[h, y0, :, sub, :, :, :] = final[sub][:, :, 3 + sub : 4 + sub, :]

    def copies(h, y0):
        to_yz, to_gx = [], []
        for j, d in enumerate(DELTAS):
            to_yz.append(
                pltpu.make_async_remote_copy(
                    src_ref=send_buf.at[h, y0],
                    dst_ref=got_yz.at[h, y0, j],
                    send_sem=send_sem.at[h, y0, j],
                    recv_sem=recv_yz.at[h, y0, j],
                    device_id=device(0, d),
                    device_id_type=MESH,
                )
            )
        for j, d in enumerate(GX_DELTAS):
            to_gx.append(
                pltpu.make_async_remote_copy(
                    src_ref=send_buf.at[h, y0],
                    dst_ref=got_gx.at[h, y0, j],
                    send_sem=send_sem.at[h, y0, 4 + j],
                    recv_sem=recv_gx.at[h, y0, j],
                    device_id=device(2 * h - 1, d),
                    device_id_type=MESH,
                )
            )
        return to_yz, to_gx

    def take_yz(h, y0):
        for j, d in enumerate(DELTAS):
            y = y0 - 2 * d
            if -4 <= y <= 5:
                put(lambda sub: got_yz[h, y0, j, :, sub], 2 * h + 2, 2, y, 1)

    def take_gx(h, y0):
        for j, d in enumerate(GX_DELTAS):
            put(lambda sub: got_gx[h, y0, j, :, sub], 6 - 6 * h, 2, y0 - 2 * d, 1)

    def half_sweep(h, carry):
        phase(h, 0)
        even_yz, even_gx = copies(h, 0)
        for copy in even_yz + even_gx:
            copy.start()
        for copy in even_yz:
            copy.wait()
        take_yz(h, 0)
        roll_all(2 * h + 2, 2)
        phase(h, 1)
        odd_yz, odd_gx = copies(h, 1)
        for copy in odd_yz + odd_gx:
            copy.start()
        for copy in even_gx + odd_yz + odd_gx:
            copy.wait()
        take_gx(h, 0)
        take_yz(h, 1)
        take_gx(h, 1)
        roll_all(2 * h + 2, 2)
        roll_all(6 - 6 * h, 2)
        return carry

    lax.fori_loop(0, 2, half_sweep, 0)

    for sub in (0, 1):
        spin_out[:, sub] = state[1, :, sub, 2:6, 4 + sub : 6 + sub, :]
    cosines(1, 6, 0)
    results = network([load_cosine(c) for c in FINAL])
    for column, value in zip(FINAL, results):
        store_slope(column, value)
    for sub in (0, 1):
        total = fields(sub, 1, 4, 1, 0)
        field_out[:, sub] = total[:, :, 3 + sub : 5 + sub, :]


def solution(mesh):
    n_gx, n_yz = mesh.shape["gx"], mesh.shape["yz"]

    def per_device(spin, pair, mix, bias, out_w):
        brick = jax.ShapeDtypeStruct(spin.shape, F32)
        vmem = pl.BlockSpec(memory_space=pltpu.VMEM)
        dma = pltpu.SemaphoreType.DMA
        return pl.pallas_call(
            functools.partial(kernel, n_gx, n_yz),
            out_shape=(brick, brick),
            in_specs=[vmem] * 5,
            out_specs=(vmem, vmem),
            scratch_shapes=[
                pltpu.VMEM((3, 3, 2, 8, 16, 128), F32),
                pltpu.VMEM((2 * NT * 8, 128), F32),
                pltpu.VMEM(((2 * NT + 2) * 8, 128), F32),
                pltpu.VMEM((256, 256), BF16),
                pltpu.VMEM((256, 256), BF16),
                pltpu.VMEM((128, 128), F32),
                pltpu.VMEM((4, 3, 2, 4, 2, 128), F32),
                pltpu.VMEM((5, 3, 2, 2, 2, 128), F32),
                pltpu.VMEM((2, 2, 3, 2, 2, 1, 128), F32),
                pltpu.VMEM((2, 2, 4, 3, 2, 2, 1, 128), F32),
                pltpu.VMEM((2, 2, 5, 3, 2, 2, 1, 128), F32),
                dma((9,)),
                dma((9,)),
                dma((2, 2, 9)),
                dma((2, 2, 4)),
                dma((2, 2, 5)),
            ],
            compiler_params=pltpu.CompilerParams(collective_id=0, has_side_effects=True),
        )(spin, pair, mix, bias.reshape(1, 128), out_w.reshape(1, 128))

    placed = (P(None, None, "gx", "yz", None), P(), P(), P(), P())
    return jax.shard_map(
        per_device,
        mesh=mesh,
        in_specs=placed,
        out_specs=(P(None, None, "gx", "yz", None), P(None, None, "gx", "yz", None)),
        check_vma=False,
    )
```

```python
import functools

import jax
import jax.numpy as jnp
from jax import lax
from jax.experimental import pallas as pl
from jax.experimental.pallas import tpu as pltpu
from jax.sharding import PartitionSpec as P

MESH = pl.DeviceIdType.MESH
NB = 8
NXI = 6
NT = 2 * NXI * 8
TIME_STEP = 0.1
CHUNK = 2
F32 = jnp.float32
BF16 = jnp.bfloat16

FIRST = [(i, j, k) for i in (-1, 0) for j in (-1, 0) for k in (-1, 0)]
SECOND = [(1, 0, 0), (-1, 0, 0), (0, 1, 0), (0, -1, 0), (0, 0, 1), (0, 0, -1)]
DELTAS = (1, -1, 2, -2)
GX_DELTAS = (0, 1, -1, 2, -2)


def bond_list(sub):
    sign = 1 - 2 * sub
    result = [(1 - sub, sign * i, sign * j, sign * k) for i, j, k in FIRST]
    return result + [(sub, i, j, k) for i, j, k in SECOND]


BONDS = (bond_list(0), bond_list(1))


def partner(o):
    return o if o < 8 else 8 + ((o - 8) ^ 1)


def row_shift(sub, target, dy):
    return dy + target - sub


def with_neighbours(atoms):
    result = set(atoms)
    for sub, x, y, z in atoms:
        for target, dx, dy, dz in BONDS[sub]:
            result.add((target, x + dx, y + dy, z + dz))
    return result


def columns_of(atoms):
    return sorted({atom[:3] for atom in atoms})


MAIN = columns_of(with_neighbours([(s, x, 0, 0) for s in (0, 1) for x in (0, 1)]))
LOW_SEED = [(1, x, -2, 63) for x in (0, 1)]
HIGH_SEED = [(0, x, 2, 0) for x in (0, 1)]
LOW_SIDE = [c for c in columns_of(with_neighbours(LOW_SEED)) if c not in MAIN]
HIGH_SIDE = [c for c in columns_of(with_neighbours(HIGH_SEED)) if c not in MAIN]
OWN = [(s, x, y, 0) for s in (0, 1) for x in range(4) for y in (0, 1)]
FINAL = columns_of(with_neighbours(OWN))


def places_of(atoms):
    return {(a[1], a[2]) for a in with_neighbours(with_neighbours(atoms))}


def phase_reads(h, y0):
    seeds = [(s, x, 0, z) for s in (0, 1) for x in (0, 1) for z in (0, 64)]
    places = places_of(seeds + LOW_SEED + HIGH_SEED)
    return {(x + 2 * h, y + y0) for x, y in places}


FINAL_READS = places_of(OWN)


def message_places(h, y0, dgx, e):
    return {(4 * dgx + 2 * h + x, y0 + 2 * e) for x in (0, 1)}


def sources(h, y0):
    later = [(h, y0, phase_reads(h, y0)) for h, y0 in PHASES[2 * h + y0 + 1 :]]
    later.append((2, 0, FINAL_READS))
    result = {}
    for dgx in (0, 1, -1):
        for e in (0, 1, -1, 2, -2):
            if (dgx, e) == (0, 0):
                continue
            for rank, (_, _, reads) in enumerate(later):
                if message_places(h, y0, dgx, e) & reads:
                    result[(dgx, e)] = 2 * h + y0 + 1 + rank
                    break
    return result


PHASES = [(0, 0), (0, 1), (1, 0), (1, 1)]
SOURCES = [sources(h, y0) for h, y0 in PHASES]
ORDERED = [sorted(found, key=lambda d: (found[d], d)) for found in SOURCES]


def tile(sub, xi, slot, half):
    return half * NT + (sub * NXI + xi) * 8 + slot


def column_tile(column, half):
    sub, x, y = column
    return tile(sub, x + 1, y + 3 + sub, half)


def rolled(value, dz):
    return value if dz == 0 else pltpu.roll(value, (-dz) % 128, value.ndim - 1)


def kernel(
    n_gx,
    n_yz,
    spin_ref,
    pair_ref,
    mix_ref,
    bias_ref,
    out_w_ref,
    spin_out,
    field_out,
    state,
    cosine,
    slope,
    first_w,
    second_w,
    scratch_w,
    start_yz,
    start_gx,
    send_buf,
    got,
    start_send,
    start_recv,
    send_sem,
    recv_sem,
):
    gx = lax.axis_index("gx")
    yz = lax.axis_index("yz")

    def device(dgx, dyz):
        return (lax.rem(gx + dgx + n_gx, n_gx), lax.rem(yz + dyz + n_yz, n_yz))

    barrier = pltpu.get_barrier_semaphore()
    partners = [(0, d) for d in DELTAS] + [(s, d) for s in (1, -1) for d in GX_DELTAS]
    for dgx, dyz in partners:
        pl.semaphore_signal(barrier, inc=1, device_id=device(dgx, dyz), device_id_type=MESH)

    scratch_w[...] = jnp.zeros((128, 128), F32)
    for k in range(NB):
        scratch_w[16 * k : 16 * k + 8, :] = pair_ref[pl.ds(k, 8, stride=8), :]
        scratch_w[16 * k + 8 : 16 * k + 14, :] = pair_ref[pl.ds(64 + k, 6, stride=8), :]
    merged = jnp.dot(
        scratch_w[...],
        mix_ref[...],
        precision=lax.Precision.HIGHEST,
        preferred_element_type=F32,
    )
    row = lax.broadcasted_iota(jnp.int32, (128, 128), 0)
    with_bias = jnp.where(row == 14, jnp.broadcast_to(bias_ref[...], (128, 128)), merged)
    degree = (row // 16 + 1).astype(F32)
    scaled = -merged * degree * jnp.broadcast_to(out_w_ref[...], (128, 128))

    def stacked(matrix):
        high = matrix.astype(BF16)
        low = (matrix - high.astype(F32)).astype(BF16)
        return jnp.concatenate(
            [jnp.concatenate([high, high], 1), jnp.concatenate([low, low], 1)], 0
        )

    first_w[...] = stacked(with_bias.T)
    second_w[...] = stacked(scaled)
    cosine[...] = jnp.ones(cosine.shape, F32)
    slope[...] = jnp.zeros(slope.shape, F32)
    state[...] = jnp.zeros(state.shape, F32)

    pl.semaphore_wait(barrier, len(partners))

    starts = []
    for j, d in enumerate(DELTAS):
        starts.append(
            pltpu.make_async_remote_copy(
                src_ref=spin_ref,
                dst_ref=start_yz.at[j],
                send_sem=start_send.at[j],
                recv_sem=start_recv.at[j],
                device_id=device(0, d),
                device_id_type=MESH,
            )
        )
    for j, d in enumerate(GX_DELTAS):
        starts.append(
            pltpu.make_async_remote_copy(
                src_ref=spin_ref.at[:, :, 2:4],
                dst_ref=start_gx.at[j],
                send_sem=start_send.at[4 + j],
                recv_sem=start_recv.at[4 + j],
                device_id=device(1, d),
                device_id_type=MESH,
            )
        )
    for copy in starts:
        copy.start()

    def put(value_of_sub, first_x, count, y, rows):
        for sub in (0, 1):
            r = y + 4 + sub
            state[1, :, sub, first_x : first_x + count, r : r + rows, :] = value_of_sub(sub)

    def roll_all(first_x, count):
        for sub in (0, 1):
            value = state[1, :, sub, first_x : first_x + count]
            state[0, :, sub, first_x : first_x + count] = rolled(value, -1)
            state[2, :, sub, first_x : first_x + count] = rolled(value, 1)

    put(lambda sub: spin_ref[:, sub], 2, 4, 0, 2)
    for copy in starts:
        copy.wait()
    for j, d in enumerate(DELTAS):
        put(lambda sub: start_yz[j, :, sub], 2, 4, -2 * d, 2)
    for j, d in enumerate(GX_DELTAS):
        put(lambda sub: start_gx[j, :, sub], 0, 2, -2 * d, 2)
    roll_all(0, 6)

    def cosines(first_x, y0, groups, touched=None):
        r0 = 1 + y0
        for sub, bonds in ((0, (0, 1, 2, 3, 4, 5, 6, 7, 8, 10, 12)), (1, (8, 10, 12))):
            for o in bonds:
                target, dx, dy, dz = BONDS[sub][o]
                mate = partner(o)
                shift = row_shift(sub, target, dy)
                wanted = [
                    xi
                    for xi in range(-1, NXI + 1)
                    if ((sub, xi) in groups or (target, xi + dx) in groups)
                    and (touched is None or xi in touched or xi + dx in touched)
                ]
                first, count = wanted[0], wanted[-1] - wanted[0] + 1
                centre = state[1, :, sub, first_x + first : first_x + first + count, r0 : r0 + 8]
                r, x = r0 + shift, first_x + first + dx
                other = state[1 + dz, :, target, x : x + count, r : r + 8]
                product = centre * other
                value = product[0] + product[1] + product[2]
                back = rolled(value, -dz)
                for xi in wanted:
                    if (sub, xi) in groups:
                        at = (tile(sub, xi, 0, o // 8) + 1) * 8 + o % 8
                        cosine[pl.ds(at, 8, stride=8), :] = value[xi - first]
                    if (target, xi + dx) in groups:
                        at = (tile(target, xi + dx, shift, mate // 8) + 1) * 8 + mate % 8
                        cosine[pl.ds(at, 8, stride=8), :] = back[xi - first]

    def load_cosine(column):
        halves = []
        for half in (0, 1):
            at = column_tile(column, half) * 8 + 8
            halves.append(cosine[at : at + 8, :])
        return jnp.concatenate(halves, 0)

    def store_slope(column, value):
        for half in (0, 1):
            at = column_tile(column, half) * 8 + 8
            slope[at : at + 8, :] = value[8 * half : 8 * half + 8, :]

    def product(weight, value):
        high = value.astype(BF16)
        low = (value - high.astype(F32)).astype(BF16)
        wide = jnp.dot(
            weight[...], jnp.concatenate([high, low], 0), preferred_element_type=F32
        )
        return wide[:128] + wide[128:]

    def network(values):
        results = []
        for begin in range(0, len(values), CHUNK):
            part = values[begin : begin + CHUNK]
            c = jnp.concatenate(part, 1)
            twice = c + c
            firsts = [jnp.ones_like(c), c]
            seconds = [jnp.ones_like(c), twice]
            for _ in range(2, NB + 1):
                firsts.append(twice * firsts[-1] - firsts[-2])
                seconds.append(twice * seconds[-1] - seconds[-2])
            u = jnp.tanh(product(first_w, jnp.concatenate(firsts[1:], 0)))
            d = product(second_w, 1.0 - u * u)
            g = d[0:16]
            for k in range(1, NB):
                g = g + d[16 * k : 16 * k + 16] * seconds[k]
            results += [g[:, 128 * j : 128 * j + 128] for j in range(len(part))]
        return results

    lane = lax.broadcasted_iota(jnp.int32, (16, 128), 1)

    def packed(groups):
        result = None
        for first, columns in groups:
            order = lax.rem(lane + (256 - first), 128)
            for m, column in enumerate(columns):
                value = load_cosine(column)
                if m:
                    value = pltpu.roll(value, 4 * m, 1)
                if result is None:
                    result = value
                else:
                    inside = (order >= 4 * m) & (order < 4 * m + 4)
                    result = jnp.where(inside, value, result)
        return result

    def packed_pair(columns):
        result = None
        low = lax.rem(lane + (256 - 63), 128)
        high = lax.rem(lane + (256 - 125), 128)
        for m, column in enumerate(columns):
            value = load_cosine(column)
            if m:
                value = pltpu.roll(value, 4 * m, 1)
                inside = ((low >= 4 * m) & (low < 4 * m + 4)) | (
                    (high >= 4 * m) & (high < 4 * m + 4)
                )
                value = jnp.where(inside, value, result)
            result = value
        return result

    def spread(value, columns):
        for m, column in enumerate(columns):
            store_slope(column, pltpu.roll(value, 128 - 4 * m, 1) if m else value)

    def fields(sub, xi0, count, first_x, y0):
        r0 = 1 + y0
        total = None
        for o, (target, dx, dy, dz) in enumerate(BONDS[sub]):
            mate = partner(o)
            shift = row_shift(sub, target, dy)
            coefficients = []
            for xi in range(xi0, xi0 + count):
                at = (tile(sub, xi, 0, o // 8) + 1) * 8 + o % 8
                own = slope[pl.ds(at, 8, stride=8), :]
                at = (tile(target, xi + dx, shift, mate // 8) + 1) * 8 + mate % 8
                theirs = slope[pl.ds(at, 8, stride=8), :]
                coefficients.append((own + rolled(theirs, dz))[None])
            coefficient = jnp.concatenate(coefficients, 0)
            spins = state[
                1 + dz,
                :,
                target,
                first_x + xi0 + dx : first_x + xi0 + dx + count,
                r0 + shift : r0 + shift + 8,
                :,
            ]
            term = coefficient[None] * spins
            total = term if total is None else total + term
        return total

    def rotate(spin, field):
        w = [TIME_STEP * field[c] for c in range(3)]
        s = [spin[c] for c in range(3)]
        square = w[0] * w[0] + w[1] * w[1] + w[2] * w[2]
        tiny = square < 1e-30
        size = jnp.sqrt(jnp.where(tiny, 1.0, square))
        sine, cosine_half = jnp.sin(0.5 * size), jnp.cos(0.5 * size)
        inverse = 1.0 / size
        half = jnp.where(tiny, 0.5, sine * inverse)
        ratio = 2.0 * half * jnp.where(tiny, 1.0, cosine_half)
        versine = 2.0 * half * half
        turn = 1.0 - versine * jnp.where(tiny, 0.0, square)
        along = versine * (w[0] * s[0] + w[1] * s[1] + w[2] * s[2])
        cross = [
            w[1] * s[2] - w[2] * s[1],
            w[2] * s[0] - w[0] * s[2],
            w[0] * s[1] - w[1] * s[0],
        ]
        return jnp.concatenate(
            [(turn * s[c] + ratio * cross[c] + along * w[c])[None] for c in range(3)], 0
        )

    shape = (3, 2, 8, 128)
    slot_of = lax.broadcasted_iota(jnp.int32, shape, 2)
    z_of = lax.broadcasted_iota(jnp.int32, shape, 3)
    seam = ((z_of >= 64) & (z_of < 66)) | (z_of >= 126)

    def write_targets(sub, first_x, y0, value):
        r0 = 1 + y0
        for dz in (-1, 0, 1):
            state[1 + dz, :, sub, first_x + 1 : first_x + 3, r0 : r0 + 8, :] = rolled(value, dz)

    def evaluate(columns):
        for column, value in zip(columns, network([load_cosine(c) for c in columns])):
            store_slope(column, value)

    def groups_of(columns):
        return {(c[0], c[1] + 1) for c in columns}

    def split(columns, arriving, origin):
        early, late = [], []
        for sub, x, y in columns:
            around = {(a[1] + origin[0], a[2] + origin[1]) for a in with_neighbours([(sub, x, y, 0)])}
            (late if around & arriving else early).append((sub, x, y))
        return early, late

    def gather(columns, first_x, y0, origin, reader):
        groups = groups_of(columns + (LOW_SIDE + HIGH_SIDE if reader < 4 else []))
        if reader == 0:
            cosines(first_x, y0, groups)
            return columns
        arriving = set()
        for p in range(reader):
            for source in ORDERED[p]:
                if SOURCES[p][source] == reader:
                    if p < reader - 1:
                        receive(p, source)
                    else:
                        arriving |= message_places(*PHASES[p], *source)
        for p in range(reader - 1):
            reroll(p, reader)
        early, late = split(columns, arriving, origin)
        cosines(first_x, y0, groups)
        evaluate(early)
        for source in ORDERED[reader - 1]:
            if SOURCES[reader - 1][source] == reader:
                receive(reader - 1, source)
        reroll(reader - 1, reader)
        touched = {x + 2 - first_x for x, _ in arriving}
        cosines(first_x, y0, groups, touched)
        return late

    def phase(h, y0):
        x0 = 2 * h
        first_x = x0 + 1
        r0 = 1 + y0
        late = gather(MAIN, first_x, y0, (x0, y0), 2 * h + y0)
        sides = packed([(62, LOW_SIDE), (126, HIGH_SIDE)])
        results = network([load_cosine(c) for c in late] + [sides])
        for column, value in zip(late, results):
            store_slope(column, value)
        spread(results[-1], LOW_SIDE)
        spread(results[-1], HIGH_SIDE)
        old, trial = [], []
        for sub in (0, 1):
            spin = state[1, :, sub, first_x + 1 : first_x + 3, r0 : r0 + 8, :]
            old.append(spin)
            trial.append(rotate(spin, fields(sub, 1, 2, first_x, y0)))
        for sub in (0, 1):
            if sub == 0:
                extra = (slot_of == 5) & (z_of == 0)
            else:
                extra = (slot_of == 2) & (z_of == 63)
            change = ((slot_of == 3 + sub) & (z_of < 64)) | extra
            write_targets(sub, first_x, y0, jnp.where(change, trial[sub], old[sub]))
        cosines(first_x, y0, groups_of(MAIN), {1, 2})
        groups = (MAIN[:9], MAIN[9:])
        results = network([packed_pair(columns) for columns in groups])
        for columns, value in zip(groups, results):
            spread(value, columns)
        final = []
        for sub in (0, 1):
            spin = state[1, :, sub, first_x + 1 : first_x + 3, r0 : r0 + 8, :]
            again = rotate(spin, fields(sub, 1, 2, first_x, y0))
            late = (slot_of == 3 + sub) & (z_of >= 64)
            final.append(jnp.where(late, jnp.where(seam, again, trial[sub]), spin))
        for sub in (0, 1):
            write_targets(sub, first_x, y0, final[sub])
            send_buf[2 * h + y0, :, sub, :, :, :] = final[sub][:, :, 3 + sub : 4 + sub, :]

    started = {}

    def send(p):
        for j, (dgx, e) in enumerate(ORDERED[p]):
            copy = pltpu.make_async_remote_copy(
                src_ref=send_buf.at[p],
                dst_ref=got.at[p, j],
                send_sem=send_sem.at[p, j],
                recv_sem=recv_sem.at[p, j],
                device_id=device(-dgx, -e),
                device_id_type=MESH,
            )
            copy.start()
            started[(p, (dgx, e))] = copy

    def receive(p, source):
        started[(p, source)].wait()
        h, y0 = PHASES[p]
        j = ORDERED[p].index(source)
        dgx, e = source
        put(lambda sub: got[p, j, :, sub], 4 * dgx + 2 * h + 2, 2, y0 + 2 * e, 1)

    def reroll(p, reader):
        h, _ = PHASES[p]
        for dgx in (0, 1, -1):
            if any(d[0] == dgx and SOURCES[p][d] == reader for d in ORDERED[p]):
                roll_all(4 * dgx + 2 * h + 2, 2)

    for p in range(4):
        phase(*PHASES[p])
        send(p)

    for sub in (0, 1):
        spin_out[:, sub] = state[1, :, sub, 2:6, 4 + sub : 6 + sub, :]
    evaluate(gather(FINAL, 1, 0, (0, 0), 4))
    for sub in (0, 1):
        total = fields(sub, 1, 4, 1, 0)
        field_out[:, sub] = total[:, :, 3 + sub : 5 + sub, :]


def solution(mesh):
    n_gx, n_yz = mesh.shape["gx"], mesh.shape["yz"]

    def per_device(spin, pair, mix, bias, out_w):
        brick = jax.ShapeDtypeStruct(spin.shape, F32)
        vmem = pl.BlockSpec(memory_space=pltpu.VMEM)
        dma = pltpu.SemaphoreType.DMA
        return pl.pallas_call(
            functools.partial(kernel, n_gx, n_yz),
            out_shape=(brick, brick),
            in_specs=[vmem] * 5,
            out_specs=(vmem, vmem),
            scratch_shapes=[
                pltpu.VMEM((3, 3, 2, 8, 16, 128), F32),
                pltpu.VMEM(((2 * NT + 2) * 8, 128), F32),
                pltpu.VMEM(((2 * NT + 2) * 8, 128), F32),
                pltpu.VMEM((256, 256), BF16),
                pltpu.VMEM((256, 256), BF16),
                pltpu.VMEM((128, 128), F32),
                pltpu.VMEM((4, 3, 2, 4, 2, 128), F32),
                pltpu.VMEM((5, 3, 2, 2, 2, 128), F32),
                pltpu.VMEM((4, 3, 2, 2, 1, 128), F32),
                pltpu.VMEM((4, 9, 3, 2, 2, 1, 128), F32),
                dma((9,)),
                dma((9,)),
                dma((4, 9)),
                dma((4, 9)),
            ],
            compiler_params=pltpu.CompilerParams(collective_id=0, has_side_effects=True),
        )(spin, pair, mix, bias.reshape(1, 128), out_w.reshape(1, 128))

    placed = (P(None, None, "gx", "yz", None), P(), P(), P(), P())
    return jax.shard_map(
        per_device,
        mesh=mesh,
        in_specs=placed,
        out_specs=(P(None, None, "gx", "yz", None), P(None, None, "gx", "yz", None)),
        check_vma=False,
    )
```

```python
import functools
import math

import jax
import jax.numpy as jnp
from jax import lax
from jax.experimental import pallas as pl
from jax.experimental.pallas import tpu as pltpu
from jax.sharding import PartitionSpec as P

MESH = pl.DeviceIdType.MESH
NB = 8
NXI = 6
TIME_STEP = 0.1
CHUNK = 2
F32 = jnp.float32
BF16 = jnp.bfloat16

FIRST = [(i, j, k) for i in (-1, 0) for j in (-1, 0) for k in (-1, 0)]
SECOND = [(1, 0, 0), (-1, 0, 0), (0, 1, 0), (0, -1, 0), (0, 0, 1), (0, 0, -1)]
DELTAS = (1, -1, 2, -2)
GX_DELTAS = (0, 1, -1, 2, -2)


def bond_list(sub):
    sign = 1 - 2 * sub
    result = [(1 - sub, sign * i, sign * j, sign * k) for i, j, k in FIRST]
    return result + [(sub, i, j, k) for i, j, k in SECOND]


BONDS = (bond_list(0), bond_list(1))


def partner(o):
    return o if o < 8 else 8 + ((o - 8) ^ 1)


def row_shift(sub, target, dy):
    return dy + target - sub


def with_neighbours(atoms):
    result = set(atoms)
    for sub, x, y, z in atoms:
        for target, dx, dy, dz in BONDS[sub]:
            result.add((target, x + dx, y + dy, z + dz))
    return result


def columns_of(atoms):
    return sorted({atom[:3] for atom in atoms})


MAIN = columns_of(with_neighbours([(s, x, 0, 0) for s in (0, 1) for x in (0, 1)]))
LOW_SEED = [(1, x, -2, 63) for x in (0, 1)]
HIGH_SEED = [(0, x, 2, 0) for x in (0, 1)]
LOW_SIDE = [c for c in columns_of(with_neighbours(LOW_SEED)) if c not in MAIN]
HIGH_SIDE = [c for c in columns_of(with_neighbours(HIGH_SEED)) if c not in MAIN]
OWN = [(s, x, y, 0) for s in (0, 1) for x in range(4) for y in (0, 1)]
FINAL = columns_of(with_neighbours(OWN))


def places_of(atoms):
    return {(a[1], a[2]) for a in with_neighbours(with_neighbours(atoms))}


def phase_reads(h, y0):
    seeds = [(s, x, 0, z) for s in (0, 1) for x in (0, 1) for z in (0, 64)]
    places = places_of(seeds + LOW_SEED + HIGH_SEED)
    return {(x + 2 * h, y + y0) for x, y in places}


FINAL_READS = places_of(OWN)


def message_places(h, y0, dgx, e):
    return {(4 * dgx + 2 * h + x, y0 + 2 * e) for x in (0, 1)}


def sources(h, y0):
    later = [(h, y0, phase_reads(h, y0)) for h, y0 in PHASES[2 * h + y0 + 1 :]]
    later.append((2, 0, FINAL_READS))
    result = {}
    for dgx in (0, 1, -1):
        for e in (0, 1, -1, 2, -2):
            if (dgx, e) == (0, 0):
                continue
            for rank, (_, _, reads) in enumerate(later):
                if message_places(h, y0, dgx, e) & reads:
                    result[(dgx, e)] = 2 * h + y0 + 1 + rank
                    break
    return result


PHASES = [(0, 0), (0, 1), (1, 0), (1, 1)]
SOURCES = [sources(h, y0) for h, y0 in PHASES]
ORDERED = [sorted(found, key=lambda d: (found[d], d)) for found in SOURCES]


def sine_cosine(x):
    n = jnp.floor(x * (2.0 / math.pi) + 0.5)
    y = ((x - n * 1.5703125) - n * 4.83751296997e-4) - n * 7.54978995489e-8
    y2 = y * y
    sine = y + y * y2 * (-1.6666654611e-1 + y2 * (8.3321608736e-3 - y2 * 1.9515295891e-4))
    cosine = 1.0 - 0.5 * y2 + y2 * y2 * (
        4.166664568298827e-2 + y2 * (-1.388731625493765e-3 + y2 * 2.443315711809948e-5)
    )
    quarter = n - 4.0 * jnp.floor(0.25 * n)
    odd = (quarter == 1.0) | (quarter == 3.0)
    first, second = jnp.where(odd, cosine, sine), jnp.where(odd, sine, cosine)
    first = jnp.where(quarter >= 2.0, -first, first)
    second = jnp.where((quarter == 1.0) | (quarter == 2.0), -second, second)
    return first, second


def exchange(rows):
    shape = rows[0].shape
    place = lax.broadcasted_iota(jnp.int32, shape, 1)
    rows = list(rows)
    for step in (4, 2, 1):
        low = (place & step) == 0
        for i in range(8):
            if i & step:
                continue
            a, b = rows[i], rows[i + step]
            rows[i] = jnp.where(low, a, pltpu.roll(b, step, 1))
            rows[i + step] = jnp.where(low, pltpu.roll(a, 8 - step, 1), b)
    return rows


def rolled(value, dz):
    return value if dz == 0 else pltpu.roll(value, (-dz) % 128, value.ndim - 1)


def kernel(
    n_gx,
    n_yz,
    spin_hbm,
    pair_hbm,
    mix_hbm,
    bias_hbm,
    out_w_hbm,
    both_out,
    state,
    cosine,
    slope,
    by_bond,
    first_w,
    second_w,
    scratch_w,
    spin_ref,
    pair_ref,
    mix_ref,
    bias_ref,
    out_w_ref,
    load_sem,
    start_yz,
    start_gx,
    send_buf,
    got,
    start_send,
    start_recv,
    send_sem,
    recv_sem,
):
    gx = lax.axis_index("gx")
    yz = lax.axis_index("yz")

    def device(dgx, dyz):
        return (lax.rem(gx + dgx + n_gx, n_gx), lax.rem(yz + dyz + n_yz, n_yz))

    barrier = pltpu.get_barrier_semaphore()
    partners = [(0, d) for d in DELTAS] + [(s, d) for s in (1, -1) for d in GX_DELTAS]
    for dgx, dyz in partners:
        pl.semaphore_signal(barrier, inc=1, device_id=device(dgx, dyz), device_id_type=MESH)

    loads = []
    for j, (source, target) in enumerate(
        (
            (spin_hbm, spin_ref),
            (pair_hbm, pair_ref),
            (mix_hbm, mix_ref),
            (bias_hbm, bias_ref),
            (out_w_hbm, out_w_ref),
        )
    ):
        load = pltpu.make_async_copy(source, target, load_sem.at[j])
        load.start()
        loads.append(load)
    slope[...] = jnp.zeros(slope.shape, F32)
    state[...] = jnp.zeros(state.shape, F32)

    pl.semaphore_wait(barrier, len(partners))

    starts = []
    for j, d in enumerate(DELTAS):
        starts.append(
            pltpu.make_async_remote_copy(
                src_ref=spin_hbm,
                dst_ref=start_yz.at[j],
                send_sem=start_send.at[j],
                recv_sem=start_recv.at[j],
                device_id=device(0, d),
                device_id_type=MESH,
            )
        )
    for j, d in enumerate(GX_DELTAS):
        starts.append(
            pltpu.make_async_remote_copy(
                src_ref=spin_hbm.at[:, :, 2:4],
                dst_ref=start_gx.at[j],
                send_sem=start_send.at[4 + j],
                recv_sem=start_recv.at[4 + j],
                device_id=device(1, d),
                device_id_type=MESH,
            )
        )
    for copy in starts:
        copy.start()

    for load in loads:
        load.wait()
    scratch_w[...] = jnp.zeros((128, 128), F32)
    for k in range(NB):
        scratch_w[16 * k : 16 * k + 8, :] = pair_ref[pl.ds(k, 8, stride=8), :]
        scratch_w[16 * k + 8 : 16 * k + 14, :] = pair_ref[pl.ds(64 + k, 6, stride=8), :]
    merged = jnp.dot(
        scratch_w[...],
        mix_ref[...],
        precision=lax.Precision.HIGHEST,
        preferred_element_type=F32,
    )
    row = lax.broadcasted_iota(jnp.int32, (128, 128), 0)
    with_bias = jnp.where(row == 14, jnp.broadcast_to(bias_ref[...], (128, 128)), merged)
    degree = (row // 16 + 1).astype(F32)
    scaled = -merged * degree * jnp.broadcast_to(out_w_ref[...], (128, 128))

    def stacked(matrix):
        high = matrix.astype(BF16)
        low = (matrix - high.astype(F32)).astype(BF16)
        return jnp.concatenate(
            [jnp.concatenate([high, high], 1), jnp.concatenate([low, low], 1)], 0
        )

    first_w[...] = stacked(0.5 * with_bias.T)
    second_w[...] = stacked(scaled)
    def put(value_of_sub, first_x, count, y, rows):
        for sub in (0, 1):
            r = y + 4 + sub
            state[1, :, sub, first_x : first_x + count, r : r + rows, :] = value_of_sub(sub)

    def roll_all(first_x, count):
        for sub in (0, 1):
            value = state[1, :, sub, first_x : first_x + count]
            state[0, :, sub, first_x : first_x + count] = rolled(value, -1)
            state[2, :, sub, first_x : first_x + count] = rolled(value, 1)

    put(lambda sub: spin_ref[:, sub], 2, 4, 0, 2)
    for copy in starts:
        copy.wait()
    for j, d in enumerate(DELTAS):
        put(lambda sub: start_yz[j, :, sub], 2, 4, -2 * d, 2)
    for j, d in enumerate(GX_DELTAS):
        put(lambda sub: start_gx[j, :, sub], 0, 2, -2 * d, 2)
    roll_all(0, 6)

    def cosines(first_x, y0, count):
        r0 = 1 + y0
        for sub in (0, 1):
            centre = state[1, :, sub, first_x : first_x + count, r0 : r0 + 8]
            for half in (0, 1):
                values = []
                for target, dx, dy, dz in BONDS[sub][8 * half : 8 * half + 8]:
                    r, x = r0 + row_shift(sub, target, dy), first_x + dx
                    product = centre * state[1 + dz, :, target, x : x + count, r : r + 8]
                    values.append(product[0] + product[1] + product[2])
                values += [jnp.ones((count, 8, 128), F32)] * (8 - len(values))
                for slot, value in enumerate(exchange(values)):
                    if 1 <= slot <= 6:
                        cosine[half, sub, 0:count, slot] = value

    def load_cosine(column):
        sub, x, y = column
        return jnp.concatenate([cosine[half, sub, x + 1, y + 3 + sub] for half in (0, 1)], 0)

    def store_slope(column, value):
        sub, x, y = column
        for half in (0, 1):
            slope[half, sub, x + 1, y + 3 + sub] = value[8 * half : 8 * half + 8, :]

    def slopes_by_bond(count):
        for sub in (0, 1):
            for half in (0, 1):
                zero = jnp.zeros((count, 8, 128), F32)
                values = [zero] + [slope[half, sub, 0:count, slot] for slot in range(1, 7)] + [zero]
                for o, value in enumerate(exchange(values)):
                    if 8 * half + o < 14:
                        by_bond[sub, 8 * half + o, 0:count, 8:16, :] = value

    def product(weight, value):
        high = value.astype(BF16)
        low = (value - high.astype(F32)).astype(BF16)
        wide = jnp.dot(
            weight[...], jnp.concatenate([high, low], 0), preferred_element_type=F32
        )
        return wide[:128] + wide[128:]

    def network(values):
        results = []
        for begin in range(0, len(values), CHUNK):
            part = values[begin : begin + CHUNK]
            c = jnp.concatenate(part, 1)
            twice = c + c
            firsts = [None, twice, twice * twice - 2.0]
            for _ in range(3, NB + 1):
                firsts.append(twice * firsts[-1] - firsts[-2])
            seconds = [None, twice, firsts[2] + 1.0]
            for k in range(3, NB):
                seconds.append(firsts[k] + seconds[k - 2])
            u = jnp.tanh(product(first_w, jnp.concatenate(firsts[1:], 0)))
            d = product(second_w, 1.0 - u * u)
            g = d[0:16]
            for k in range(1, NB):
                g = g + d[16 * k : 16 * k + 16] * seconds[k]
            results += [g[:, 128 * j : 128 * j + 128] for j in range(len(part))]
        return results

    lane = lax.broadcasted_iota(jnp.int32, (16, 128), 1)

    def packed(groups):
        result = None
        for first, columns in groups:
            order = (lane + (256 - first)) & 127
            for m, column in enumerate(columns):
                value = load_cosine(column)
                if m:
                    value = pltpu.roll(value, 4 * m, 1)
                if result is None:
                    result = value
                else:
                    inside = (order >= 4 * m) & (order < 4 * m + 4)
                    result = jnp.where(inside, value, result)
        return result

    def packed_pair(columns):
        result = None
        low = (lane + (256 - 63)) & 127
        high = (lane + (256 - 125)) & 127
        for m, column in enumerate(columns):
            value = load_cosine(column)
            if m:
                value = pltpu.roll(value, 4 * m, 1)
                inside = ((low >= 4 * m) & (low < 4 * m + 4)) | (
                    (high >= 4 * m) & (high < 4 * m + 4)
                )
                value = jnp.where(inside, value, result)
            result = value
        return result

    def spread(value, columns):
        for m, column in enumerate(columns):
            store_slope(column, pltpu.roll(value, 128 - 4 * m, 1) if m else value)

    def fields(sub, xi0, count, first_x, y0):
        r0 = 1 + y0
        total = None
        for o, (target, dx, dy, dz) in enumerate(BONDS[sub]):
            shift = row_shift(sub, target, dy)
            own = by_bond[sub, o, xi0 : xi0 + count, 8:16, :]
            r, xi = 8 + shift, xi0 + dx
            theirs = by_bond[target, partner(o), xi : xi + count, r : r + 8, :]
            coefficient = own + rolled(theirs, dz)
            spins = state[
                1 + dz,
                :,
                target,
                first_x + xi0 + dx : first_x + xi0 + dx + count,
                r0 + shift : r0 + shift + 8,
                :,
            ]
            term = coefficient[None] * spins
            total = term if total is None else total + term
        return total

    def rotate(spin, field):
        w = [TIME_STEP * field[c] for c in range(3)]
        s = [spin[c] for c in range(3)]
        square = w[0] * w[0] + w[1] * w[1] + w[2] * w[2]
        tiny = square < 1e-30
        size = jnp.sqrt(jnp.where(tiny, 1.0, square))
        sine, cosine_half = sine_cosine(0.5 * size)
        inverse = 1.0 / size
        half = jnp.where(tiny, 0.5, sine * inverse)
        ratio = 2.0 * half * jnp.where(tiny, 1.0, cosine_half)
        versine = 2.0 * half * half
        turn = 1.0 - versine * jnp.where(tiny, 0.0, square)
        along = versine * (w[0] * s[0] + w[1] * s[1] + w[2] * s[2])
        cross = [
            w[1] * s[2] - w[2] * s[1],
            w[2] * s[0] - w[0] * s[2],
            w[0] * s[1] - w[1] * s[0],
        ]
        return jnp.concatenate(
            [(turn * s[c] + ratio * cross[c] + along * w[c])[None] for c in range(3)], 0
        )

    shape = (3, 2, 8, 128)
    slot_of = lax.broadcasted_iota(jnp.int32, shape, 2)
    z_of = lax.broadcasted_iota(jnp.int32, shape, 3)
    seam = ((z_of >= 64) & (z_of < 66)) | (z_of >= 126)

    def write_targets(sub, first_x, y0, value):
        r0 = 1 + y0
        for dz in (-1, 0, 1):
            state[1 + dz, :, sub, first_x + 1 : first_x + 3, r0 : r0 + 8, :] = rolled(value, dz)

    def evaluate(columns):
        for column, value in zip(columns, network([load_cosine(c) for c in columns])):
            store_slope(column, value)

    def split(columns, arriving, origin):
        early, late = [], []
        for sub, x, y in columns:
            around = {(a[1] + origin[0], a[2] + origin[1]) for a in with_neighbours([(sub, x, y, 0)])}
            (late if around & arriving else early).append((sub, x, y))
        return early, late

    def gather(columns, first_x, y0, origin, reader):
        count = 4 if reader < 4 else NXI
        if reader == 0:
            cosines(first_x, y0, count)
            return columns
        arriving = set()
        for p in range(reader):
            for source in ORDERED[p]:
                if SOURCES[p][source] == reader:
                    if p < reader - 1:
                        receive(p, source)
                    else:
                        arriving |= message_places(*PHASES[p], *source)
        for p in range(reader - 1):
            reroll(p, reader)
        early, late = split(columns, arriving, origin)
        cosines(first_x, y0, count)
        evaluate(early)
        for source in ORDERED[reader - 1]:
            if SOURCES[reader - 1][source] == reader:
                receive(reader - 1, source)
        reroll(reader - 1, reader)
        cosines(first_x, y0, count)
        return late

    def phase(h, y0):
        x0 = 2 * h
        first_x = x0 + 1
        r0 = 1 + y0
        late = gather(MAIN, first_x, y0, (x0, y0), 2 * h + y0)
        sides = packed([(62, LOW_SIDE), (126, HIGH_SIDE)])
        results = network([load_cosine(c) for c in late] + [sides])
        for column, value in zip(late, results):
            store_slope(column, value)
        spread(results[-1], LOW_SIDE)
        spread(results[-1], HIGH_SIDE)
        slopes_by_bond(4)
        old, trial = [], []
        for sub in (0, 1):
            spin = state[1, :, sub, first_x + 1 : first_x + 3, r0 : r0 + 8, :]
            old.append(spin)
            trial.append(rotate(spin, fields(sub, 1, 2, first_x, y0)))
        for sub in (0, 1):
            if sub == 0:
                extra = (slot_of == 5) & (z_of == 0)
            else:
                extra = (slot_of == 2) & (z_of == 63)
            change = ((slot_of == 3 + sub) & (z_of < 64)) | extra
            write_targets(sub, first_x, y0, jnp.where(change, trial[sub], old[sub]))
        cosines(first_x, y0, 4)
        groups = (MAIN[:9], MAIN[9:])
        results = network([packed_pair(columns) for columns in groups])
        for columns, value in zip(groups, results):
            spread(value, columns)
        slopes_by_bond(4)
        final = []
        for sub in (0, 1):
            spin = state[1, :, sub, first_x + 1 : first_x + 3, r0 : r0 + 8, :]
            again = rotate(spin, fields(sub, 1, 2, first_x, y0))
            late = (slot_of == 3 + sub) & (z_of >= 64)
            final.append(jnp.where(late, jnp.where(seam, again, trial[sub]), spin))
        for sub in (0, 1):
            send_buf[2 * h + y0, :, sub, :, :, :] = final[sub][:, :, 3 + sub : 4 + sub, :]
        send(2 * h + y0)
        for sub in (0, 1):
            write_targets(sub, first_x, y0, final[sub])

    started = {}

    def send(p):
        for j, (dgx, e) in enumerate(ORDERED[p]):
            copy = pltpu.make_async_remote_copy(
                src_ref=send_buf.at[p],
                dst_ref=got.at[p, j],
                send_sem=send_sem.at[p, j],
                recv_sem=recv_sem.at[p, j],
                device_id=device(-dgx, -e),
                device_id_type=MESH,
            )
            copy.start()
            started[(p, (dgx, e))] = copy

    def receive(p, source):
        started[(p, source)].wait()
        h, y0 = PHASES[p]
        j = ORDERED[p].index(source)
        dgx, e = source
        put(lambda sub: got[p, j, :, sub], 4 * dgx + 2 * h + 2, 2, y0 + 2 * e, 1)

    def reroll(p, reader):
        h, _ = PHASES[p]
        for dgx in (0, 1, -1):
            if any(d[0] == dgx and SOURCES[p][d] == reader for d in ORDERED[p]):
                roll_all(4 * dgx + 2 * h + 2, 2)

    for p in range(4):
        phase(*PHASES[p])

    for sub in (0, 1):
        both_out[0, :, sub] = state[1, :, sub, 2:6, 4 + sub : 6 + sub, :]
    evaluate(gather(FINAL, 1, 0, (0, 0), 4))
    slopes_by_bond(NXI)
    for sub in (0, 1):
        total = fields(sub, 1, 4, 1, 0)
        both_out[1, :, sub] = total[:, :, 3 + sub : 5 + sub, :]


def solution(mesh):
    n_gx, n_yz = mesh.shape["gx"], mesh.shape["yz"]

    def per_device(spin, pair, mix, bias, out_w):
        brick = jax.ShapeDtypeStruct(spin.shape, F32)
        vmem = pl.BlockSpec(memory_space=pltpu.VMEM)
        dma = pltpu.SemaphoreType.DMA
        both = pl.pallas_call(
            functools.partial(kernel, n_gx, n_yz),
            out_shape=jax.ShapeDtypeStruct((2,) + spin.shape, F32),
            in_specs=[pl.BlockSpec(memory_space=pl.ANY)] * 5,
            out_specs=vmem,
            scratch_shapes=[
                pltpu.VMEM((3, 3, 2, 8, 16, 128), F32),
                pltpu.VMEM((2, 2, NXI, 8, 8, 128), F32),
                pltpu.VMEM((2, 2, NXI, 8, 8, 128), F32),
                pltpu.VMEM((2, 14, NXI, 24, 128), F32),
                pltpu.VMEM((256, 256), BF16),
                pltpu.VMEM((256, 256), BF16),
                pltpu.VMEM((128, 128), F32),
                pltpu.VMEM(spin.shape, F32),
                pltpu.VMEM(pair.shape, F32),
                pltpu.VMEM(mix.shape, F32),
                pltpu.VMEM((1, 128), F32),
                pltpu.VMEM((1, 128), F32),
                dma((5,)),
                pltpu.VMEM((4, 3, 2, 4, 2, 128), F32),
                pltpu.VMEM((5, 3, 2, 2, 2, 128), F32),
                pltpu.VMEM((4, 3, 2, 2, 1, 128), F32),
                pltpu.VMEM((4, 9, 3, 2, 2, 1, 128), F32),
                dma((9,)),
                dma((9,)),
                dma((4, 9)),
                dma((4, 9)),
            ],
            compiler_params=pltpu.CompilerParams(collective_id=0, has_side_effects=True),
        )(spin, pair, mix, bias.reshape(1, 128), out_w.reshape(1, 128))
        return both[0], both[1]

    placed = (P(None, None, "gx", "yz", None), P(), P(), P(), P())
    return jax.shard_map(
        per_device,
        mesh=mesh,
        in_specs=placed,
        out_specs=(P(None, None, "gx", "yz", None), P(None, None, "gx", "yz", None)),
        check_vma=False,
    )
```

```python
import functools
import math

import jax
import jax.numpy as jnp
from jax import lax
from jax.experimental import pallas as pl
from jax.experimental.pallas import tpu as pltpu
from jax.sharding import PartitionSpec as P

MESH = pl.DeviceIdType.MESH
NB = 8
NXI = 6
TIME_STEP = 0.1
CHUNK = 2
F32 = jnp.float32
BF16 = jnp.bfloat16

FIRST = [(i, j, k) for i in (-1, 0) for j in (-1, 0) for k in (-1, 0)]
SECOND = [(1, 0, 0), (-1, 0, 0), (0, 1, 0), (0, -1, 0), (0, 0, 1), (0, 0, -1)]
DELTAS = (1, -1, 2, -2)
GX_DELTAS = (0, 1, -1, 2, -2)


def bond_list(sub):
    sign = 1 - 2 * sub
    result = [(1 - sub, sign * i, sign * j, sign * k) for i, j, k in FIRST]
    return result + [(sub, i, j, k) for i, j, k in SECOND]


BONDS = (bond_list(0), bond_list(1))


def partner(o):
    return o if o < 8 else 8 + ((o - 8) ^ 1)


def row_shift(sub, target, dy):
    return dy + target - sub


def with_neighbours(atoms):
    result = set(atoms)
    for sub, x, y, z in atoms:
        for target, dx, dy, dz in BONDS[sub]:
            result.add((target, x + dx, y + dy, z + dz))
    return result


def columns_of(atoms):
    return sorted({atom[:3] for atom in atoms})


MAIN = columns_of(with_neighbours([(s, x, 0, 0) for s in (0, 1) for x in (0, 1)]))
LOW_SEED = [(1, x, -2, 63) for x in (0, 1)]
HIGH_SEED = [(0, x, 2, 0) for x in (0, 1)]
LOW_SIDE = [c for c in columns_of(with_neighbours(LOW_SEED)) if c not in MAIN]
HIGH_SIDE = [c for c in columns_of(with_neighbours(HIGH_SEED)) if c not in MAIN]
OWN = [(s, x, y, 0) for s in (0, 1) for x in range(4) for y in (0, 1)]
FINAL = columns_of(with_neighbours(OWN))


def places_of(atoms):
    return {(a[1], a[2]) for a in with_neighbours(with_neighbours(atoms))}


def phase_reads(h, y0):
    seeds = [(s, x, 0, z) for s in (0, 1) for x in (0, 1) for z in (0, 64)]
    places = places_of(seeds + LOW_SEED + HIGH_SEED)
    return {(x + 2 * h, y + y0) for x, y in places}


FINAL_READS = places_of(OWN)


def message_places(h, y0, dgx, e):
    return {(4 * dgx + 2 * h + x, y0 + 2 * e) for x in (0, 1)}


def sources(h, y0):
    later = [(h, y0, phase_reads(h, y0)) for h, y0 in PHASES[2 * h + y0 + 1 :]]
    later.append((2, 0, FINAL_READS))
    result = {}
    for dgx in (0, 1, -1):
        for e in (0, 1, -1, 2, -2):
            if (dgx, e) == (0, 0):
                continue
            for rank, (_, _, reads) in enumerate(later):
                if message_places(h, y0, dgx, e) & reads:
                    result[(dgx, e)] = 2 * h + y0 + 1 + rank
                    break
    return result


PHASES = [(0, 0), (0, 1), (1, 0), (1, 1)]
SOURCES = [sources(h, y0) for h, y0 in PHASES]
ORDERED = [sorted(found, key=lambda d: (found[d], d)) for found in SOURCES]


def sine_cosine(x):
    n = jnp.floor(x * (2.0 / math.pi) + 0.5)
    y = ((x - n * 1.5703125) - n * 4.83751296997e-4) - n * 7.54978995489e-8
    y2 = y * y
    sine = y + y * y2 * (-1.6666654611e-1 + y2 * (8.3321608736e-3 - y2 * 1.9515295891e-4))
    cosine = 1.0 - 0.5 * y2 + y2 * y2 * (
        4.166664568298827e-2 + y2 * (-1.388731625493765e-3 + y2 * 2.443315711809948e-5)
    )
    quarter = n - 4.0 * jnp.floor(0.25 * n)
    odd = (quarter == 1.0) | (quarter == 3.0)
    first, second = jnp.where(odd, cosine, sine), jnp.where(odd, sine, cosine)
    first = jnp.where(quarter >= 2.0, -first, first)
    second = jnp.where((quarter == 1.0) | (quarter == 2.0), -second, second)
    return first, second


def exchange(rows):
    shape = rows[0].shape
    place = lax.broadcasted_iota(jnp.int32, shape, 1)
    rows = list(rows)
    for step in (4, 2, 1):
        low = (place & step) == 0
        for i in range(8):
            if i & step:
                continue
            a, b = rows[i], rows[i + step]
            rows[i] = jnp.where(low, a, pltpu.roll(b, step, 1))
            rows[i + step] = jnp.where(low, pltpu.roll(a, 8 - step, 1), b)
    return rows


def rolled(value, dz):
    return value if dz == 0 else pltpu.roll(value, (-dz) % 128, value.ndim - 1)


def kernel(
    n_gx,
    n_yz,
    spin_hbm,
    pair_hbm,
    mix_hbm,
    bias_hbm,
    out_w_hbm,
    both_out,
    state,
    cosine,
    slope,
    by_bond,
    first_w,
    second_w,
    scratch_w,
    spin_ref,
    pair_ref,
    mix_ref,
    bias_ref,
    out_w_ref,
    load_sem,
    start_yz,
    start_gx,
    send_buf,
    got,
    start_send,
    start_recv,
    send_sem,
    recv_sem,
):
    gx = lax.axis_index("gx")
    yz = lax.axis_index("yz")

    def device(dgx, dyz):
        return (lax.rem(gx + dgx + n_gx, n_gx), lax.rem(yz + dyz + n_yz, n_yz))

    barrier = pltpu.get_barrier_semaphore()
    partners = [(0, d) for d in DELTAS] + [(s, d) for s in (1, -1) for d in GX_DELTAS]
    for dgx, dyz in partners:
        pl.semaphore_signal(barrier, inc=1, device_id=device(dgx, dyz), device_id_type=MESH)

    loads = []
    for j, (source, target) in enumerate(
        (
            (spin_hbm, spin_ref),
            (pair_hbm, pair_ref),
            (mix_hbm, mix_ref),
            (bias_hbm, bias_ref),
            (out_w_hbm, out_w_ref),
        )
    ):
        load = pltpu.make_async_copy(source, target, load_sem.at[j])
        load.start()
        loads.append(load)
    slope[...] = jnp.zeros(slope.shape, F32)
    state[...] = jnp.zeros(state.shape, F32)

    pl.semaphore_wait(barrier, len(partners))

    starts = []
    for j, d in enumerate(DELTAS):
        starts.append(
            pltpu.make_async_remote_copy(
                src_ref=spin_hbm,
                dst_ref=start_yz.at[j],
                send_sem=start_send.at[j],
                recv_sem=start_recv.at[j],
                device_id=device(0, d),
                device_id_type=MESH,
            )
        )
    for j, d in enumerate(GX_DELTAS):
        starts.append(
            pltpu.make_async_remote_copy(
                src_ref=spin_hbm.at[:, :, 2:4],
                dst_ref=start_gx.at[j],
                send_sem=start_send.at[4 + j],
                recv_sem=start_recv.at[4 + j],
                device_id=device(1, d),
                device_id_type=MESH,
            )
        )
    for copy in starts:
        copy.start()

    for load in loads:
        load.wait()
    scratch_w[...] = jnp.zeros((128, 128), F32)
    for k in range(NB):
        scratch_w[16 * k : 16 * k + 8, :] = pair_ref[pl.ds(k, 8, stride=8), :]
        scratch_w[16 * k + 8 : 16 * k + 14, :] = pair_ref[pl.ds(64 + k, 6, stride=8), :]
    merged = jnp.dot(
        scratch_w[...],
        mix_ref[...],
        precision=lax.Precision.HIGHEST,
        preferred_element_type=F32,
    )
    row = lax.broadcasted_iota(jnp.int32, (128, 128), 0)
    with_bias = jnp.where(row == 14, jnp.broadcast_to(bias_ref[...], (128, 128)), merged)
    degree = (row // 16 + 1).astype(F32)
    scaled = -merged * degree * jnp.broadcast_to(out_w_ref[...], (128, 128))

    def stacked(matrix):
        high = matrix.astype(BF16)
        low = (matrix - high.astype(F32)).astype(BF16)
        return jnp.concatenate(
            [jnp.concatenate([high, high], 1), jnp.concatenate([low, low], 1)], 0
        )

    first_w[...] = stacked(0.5 * with_bias.T)
    second_w[...] = stacked(scaled)
    def put(value_of_sub, first_x, count, y, rows):
        for sub in (0, 1):
            r = y + 4 + sub
            state[1, :, sub, first_x : first_x + count, r : r + rows, :] = value_of_sub(sub)

    def roll_all(first_x, count):
        for sub in (0, 1):
            value = state[1, :, sub, first_x : first_x + count]
            state[0, :, sub, first_x : first_x + count] = rolled(value, -1)
            state[2, :, sub, first_x : first_x + count] = rolled(value, 1)

    put(lambda sub: spin_ref[:, sub], 2, 4, 0, 2)
    for copy in starts:
        copy.wait()
    for j, d in enumerate(DELTAS):
        put(lambda sub: start_yz[j, :, sub], 2, 4, -2 * d, 2)
    for j, d in enumerate(GX_DELTAS):
        put(lambda sub: start_gx[j, :, sub], 0, 2, -2 * d, 2)
    roll_all(0, 6)

    def cosines(first_x, y0, low, high):
        r0, count = 1 + y0, high - low
        for sub in (0, 1):
            centre = state[1, :, sub, first_x + low : first_x + high, r0 : r0 + 8]
            for half in (0, 1):
                values = []
                for target, dx, dy, dz in BONDS[sub][8 * half : 8 * half + 8]:
                    r, x = r0 + row_shift(sub, target, dy), first_x + low + dx
                    product = centre * state[1 + dz, :, target, x : x + count, r : r + 8]
                    values.append(product[0] + product[1] + product[2])
                values += [jnp.ones((count, 8, 128), F32)] * (8 - len(values))
                for slot, value in enumerate(exchange(values)):
                    if 1 <= slot <= 6:
                        cosine[half, sub, low:high, slot] = value

    def load_cosine(column):
        sub, x, y = column
        return jnp.concatenate([cosine[half, sub, x + 1, y + 3 + sub] for half in (0, 1)], 0)

    def store_slope(column, value):
        sub, x, y = column
        for half in (0, 1):
            slope[half, sub, x + 1, y + 3 + sub] = value[8 * half : 8 * half + 8, :]

    def slopes_by_bond(count):
        for sub in (0, 1):
            for half, low, high in ((0, 1 - sub, count - sub), (1, 1, count - 1)):
                zero = jnp.zeros((high - low, 8, 128), F32)
                values = [slope[half, sub, low:high, slot] for slot in range(1, 7)]
                for o, value in enumerate(exchange([zero] + values + [zero])):
                    if 8 * half + o < 14:
                        by_bond[sub, 8 * half + o, low:high, 8:16, :] = value
            for o, xi in ((0, 0), (1, count - 1)):
                for slot in range(1, 7):
                    by_bond[sub, 8 + o, xi, 8 + slot : 9 + slot, :] = slope[
                        1, sub, xi, slot, o : o + 1, :
                    ]

    def product(weight, value):
        high = value.astype(BF16)
        low = (value - high.astype(F32)).astype(BF16)
        wide = jnp.dot(
            weight[...], jnp.concatenate([high, low], 0), preferred_element_type=F32
        )
        return wide[:128] + wide[128:]

    def network(values):
        results = []
        for begin in range(0, len(values), CHUNK):
            part = values[begin : begin + CHUNK]
            c = jnp.concatenate(part, 1)
            twice = c + c
            firsts = [None, twice, twice * twice - 2.0]
            for _ in range(3, NB + 1):
                firsts.append(twice * firsts[-1] - firsts[-2])
            seconds = [None, twice, firsts[2] + 1.0]
            for k in range(3, NB):
                seconds.append(firsts[k] + seconds[k - 2])
            u = jnp.tanh(product(first_w, jnp.concatenate(firsts[1:], 0)))
            d = product(second_w, 1.0 - u * u)
            g = d[0:16]
            for k in range(1, NB):
                g = g + d[16 * k : 16 * k + 16] * seconds[k]
            results += [g[:, 128 * j : 128 * j + 128] for j in range(len(part))]
        return results

    lane = lax.broadcasted_iota(jnp.int32, (16, 128), 1)

    def packed(groups):
        result = None
        for first, columns in groups:
            order = (lane + (256 - first)) & 127
            for m, column in enumerate(columns):
                value = load_cosine(column)
                if m:
                    value = pltpu.roll(value, 4 * m, 1)
                if result is None:
                    result = value
                else:
                    inside = (order >= 4 * m) & (order < 4 * m + 4)
                    result = jnp.where(inside, value, result)
        return result

    def packed_pair(columns):
        result = None
        low = (lane + (256 - 63)) & 127
        high = (lane + (256 - 125)) & 127
        for m, column in enumerate(columns):
            value = load_cosine(column)
            if m:
                value = pltpu.roll(value, 4 * m, 1)
                inside = ((low >= 4 * m) & (low < 4 * m + 4)) | (
                    (high >= 4 * m) & (high < 4 * m + 4)
                )
                value = jnp.where(inside, value, result)
            result = value
        return result

    def spread(value, columns):
        for m, column in enumerate(columns):
            store_slope(column, pltpu.roll(value, 128 - 4 * m, 1) if m else value)

    def fields(sub, xi0, count, first_x, y0):
        r0 = 1 + y0
        total = None
        for o, (target, dx, dy, dz) in enumerate(BONDS[sub]):
            shift = row_shift(sub, target, dy)
            own = by_bond[sub, o, xi0 : xi0 + count, 8:16, :]
            r, xi = 8 + shift, xi0 + dx
            theirs = by_bond[target, partner(o), xi : xi + count, r : r + 8, :]
            coefficient = own + rolled(theirs, dz)
            spins = state[
                1 + dz,
                :,
                target,
                first_x + xi0 + dx : first_x + xi0 + dx + count,
                r0 + shift : r0 + shift + 8,
                :,
            ]
            term = coefficient[None] * spins
            total = term if total is None else total + term
        return total

    def rotate(spin, field):
        w = [TIME_STEP * field[c] for c in range(3)]
        s = [spin[c] for c in range(3)]
        square = w[0] * w[0] + w[1] * w[1] + w[2] * w[2]
        tiny = square < 1e-30
        size = jnp.sqrt(jnp.where(tiny, 1.0, square))
        sine, cosine_half = sine_cosine(0.5 * size)
        inverse = 1.0 / size
        half = jnp.where(tiny, 0.5, sine * inverse)
        ratio = 2.0 * half * jnp.where(tiny, 1.0, cosine_half)
        versine = 2.0 * half * half
        turn = 1.0 - versine * jnp.where(tiny, 0.0, square)
        along = versine * (w[0] * s[0] + w[1] * s[1] + w[2] * s[2])
        cross = [
            w[1] * s[2] - w[2] * s[1],
            w[2] * s[0] - w[0] * s[2],
            w[0] * s[1] - w[1] * s[0],
        ]
        return jnp.concatenate(
            [(turn * s[c] + ratio * cross[c] + along * w[c])[None] for c in range(3)], 0
        )

    shape = (3, 2, 8, 128)
    slot_of = lax.broadcasted_iota(jnp.int32, shape, 2)
    z_of = lax.broadcasted_iota(jnp.int32, shape, 3)
    seam = ((z_of >= 64) & (z_of < 66)) | (z_of >= 126)

    def write_targets(sub, first_x, y0, value):
        r0 = 1 + y0
        for dz in (-1, 0, 1):
            state[1 + dz, :, sub, first_x + 1 : first_x + 3, r0 : r0 + 8, :] = rolled(value, dz)

    def evaluate(columns):
        for column, value in zip(columns, network([load_cosine(c) for c in columns])):
            store_slope(column, value)

    def split(columns, arriving, origin):
        early, late = [], []
        for sub, x, y in columns:
            around = {(a[1] + origin[0], a[2] + origin[1]) for a in with_neighbours([(sub, x, y, 0)])}
            (late if around & arriving else early).append((sub, x, y))
        return early, late

    def gather(columns, first_x, y0, origin, reader):
        count = 4 if reader < 4 else NXI
        cosines_of = functools.partial(cosines, first_x, y0)
        if reader == 0:
            cosines_of(0, count)
            return columns
        for p in range(reader - 1):
            for source in ORDERED[p]:
                if SOURCES[p][source] == reader:
                    receive(p, source)
            reroll(p, reader, (0, 1, -1))
        p = reader - 1
        tiers = []
        late = [d for d in ORDERED[p] if SOURCES[p][d] == reader]
        if reader in (1, 3):
            parts = ([(0, 1)], [d for d in late if d != (0, 1)])
        else:
            parts = ([d for d in late if d[0] == 0], [d for d in late if d[0] != 0])
        for found in parts:
            places = set().union(*[message_places(*PHASES[p], *d) for d in found])
            tiers.append((found, places, {d[0] for d in found}))
        cosines_of(0, count)
        for step, (found, places, sides) in enumerate(tiers):
            ready, columns = split(columns, set().union(*[t[1] for t in tiers[step:]]), origin)
            evaluate(ready)
            for source in found:
                receive(p, source)
            reroll(p, reader, sides)
            touched = [x + 2 - first_x for x, _ in places]
            cosines_of(max(0, min(touched) - 1), min(count, max(touched) + 2))
        return columns

    def phase(h, y0):
        x0 = 2 * h
        first_x = x0 + 1
        r0 = 1 + y0
        late = gather(MAIN, first_x, y0, (x0, y0), 2 * h + y0)
        sides = packed([(62, LOW_SIDE), (126, HIGH_SIDE)])
        results = network([load_cosine(c) for c in late] + [sides])
        for column, value in zip(late, results):
            store_slope(column, value)
        spread(results[-1], LOW_SIDE)
        spread(results[-1], HIGH_SIDE)
        slopes_by_bond(4)
        old, trial = [], []
        for sub in (0, 1):
            spin = state[1, :, sub, first_x + 1 : first_x + 3, r0 : r0 + 8, :]
            old.append(spin)
            trial.append(rotate(spin, fields(sub, 1, 2, first_x, y0)))
        for sub in (0, 1):
            if sub == 0:
                extra = (slot_of == 5) & (z_of == 0)
            else:
                extra = (slot_of == 2) & (z_of == 63)
            change = ((slot_of == 3 + sub) & (z_of < 64)) | extra
            write_targets(sub, first_x, y0, jnp.where(change, trial[sub], old[sub]))
        cosines(first_x, y0, 0, 4)
        groups = (MAIN[:9], MAIN[9:])
        results = network([packed_pair(columns) for columns in groups])
        for columns, value in zip(groups, results):
            spread(value, columns)
        slopes_by_bond(4)
        final = []
        for sub in (0, 1):
            spin = state[1, :, sub, first_x + 1 : first_x + 3, r0 : r0 + 8, :]
            again = rotate(spin, fields(sub, 1, 2, first_x, y0))
            late = (slot_of == 3 + sub) & (z_of >= 64)
            final.append(jnp.where(late, jnp.where(seam, again, trial[sub]), spin))
        for sub in (0, 1):
            send_buf[2 * h + y0, :, sub, :, :, :] = final[sub][:, :, 3 + sub : 4 + sub, :]
        send(2 * h + y0)
        for sub in (0, 1):
            write_targets(sub, first_x, y0, final[sub])

    started = {}

    def send(p):
        for j, (dgx, e) in enumerate(ORDERED[p]):
            copy = pltpu.make_async_remote_copy(
                src_ref=send_buf.at[p],
                dst_ref=got.at[p, j],
                send_sem=send_sem.at[p, j],
                recv_sem=recv_sem.at[p, j],
                device_id=device(-dgx, -e),
                device_id_type=MESH,
            )
            copy.start()
            started[(p, (dgx, e))] = copy

    def receive(p, source):
        started[(p, source)].wait()
        h, y0 = PHASES[p]
        j = ORDERED[p].index(source)
        dgx, e = source
        put(lambda sub: got[p, j, :, sub], 4 * dgx + 2 * h + 2, 2, y0 + 2 * e, 1)

    def reroll(p, reader, sides):
        h, _ = PHASES[p]
        for dgx in sides:
            if any(d[0] == dgx and SOURCES[p][d] == reader for d in ORDERED[p]):
                roll_all(4 * dgx + 2 * h + 2, 2)

    for p in range(4):
        phase(*PHASES[p])

    for sub in (0, 1):
        both_out[0, :, sub] = state[1, :, sub, 2:6, 4 + sub : 6 + sub, :]
    evaluate(gather(FINAL, 1, 0, (0, 0), 4))
    slopes_by_bond(NXI)
    for sub in (0, 1):
        total = fields(sub, 1, 4, 1, 0)
        both_out[1, :, sub] = total[:, :, 3 + sub : 5 + sub, :]


def solution(mesh):
    n_gx, n_yz = mesh.shape["gx"], mesh.shape["yz"]

    def per_device(spin, pair, mix, bias, out_w):
        brick = jax.ShapeDtypeStruct(spin.shape, F32)
        vmem = pl.BlockSpec(memory_space=pltpu.VMEM)
        dma = pltpu.SemaphoreType.DMA
        both = pl.pallas_call(
            functools.partial(kernel, n_gx, n_yz),
            out_shape=jax.ShapeDtypeStruct((2,) + spin.shape, F32),
            in_specs=[pl.BlockSpec(memory_space=pl.ANY)] * 5,
            out_specs=vmem,
            scratch_shapes=[
                pltpu.VMEM((3, 3, 2, 8, 16, 128), F32),
                pltpu.VMEM((2, 2, NXI, 8, 8, 128), F32),
                pltpu.VMEM((2, 2, NXI, 8, 8, 128), F32),
                pltpu.VMEM((2, 14, NXI, 24, 128), F32),
                pltpu.VMEM((256, 256), BF16),
                pltpu.VMEM((256, 256), BF16),
                pltpu.VMEM((128, 128), F32),
                pltpu.VMEM(spin.shape, F32),
                pltpu.VMEM(pair.shape, F32),
                pltpu.VMEM(mix.shape, F32),
                pltpu.VMEM((1, 128), F32),
                pltpu.VMEM((1, 128), F32),
                dma((5,)),
                pltpu.VMEM((4, 3, 2, 4, 2, 128), F32),
                pltpu.VMEM((5, 3, 2, 2, 2, 128), F32),
                pltpu.VMEM((4, 3, 2, 2, 1, 128), F32),
                pltpu.VMEM((4, 9, 3, 2, 2, 1, 128), F32),
                dma((9,)),
                dma((9,)),
                dma((4, 9)),
                dma((4, 9)),
            ],
            compiler_params=pltpu.CompilerParams(collective_id=0, has_side_effects=True),
        )(spin, pair, mix, bias.reshape(1, 128), out_w.reshape(1, 128))
        return both[0], both[1]

    placed = (P(None, None, "gx", "yz", None), P(), P(), P(), P())
    return jax.shard_map(
        per_device,
        mesh=mesh,
        in_specs=placed,
        out_specs=(P(None, None, "gx", "yz", None), P(None, None, "gx", "yz", None)),
        check_vma=False,
    )
```

```python
import functools
import math

import jax
import jax.numpy as jnp
from jax import lax
from jax.experimental import pallas as pl
from jax.experimental.pallas import tpu as pltpu
from jax.sharding import PartitionSpec as P

MESH = pl.DeviceIdType.MESH
NB = 8
NXI = 6
TIME_STEP = 0.1
CHUNK = 20
F32 = jnp.float32
BF16 = jnp.bfloat16

FIRST = [(i, j, k) for i in (-1, 0) for j in (-1, 0) for k in (-1, 0)]
SECOND = [(1, 0, 0), (-1, 0, 0), (0, 1, 0), (0, -1, 0), (0, 0, 1), (0, 0, -1)]
DELTAS = (1, -1, 2, -2)
GX_DELTAS = (0, 1, -1, 2, -2)


def bond_list(sub):
    sign = 1 - 2 * sub
    result = [(1 - sub, sign * i, sign * j, sign * k) for i, j, k in FIRST]
    return result + [(sub, i, j, k) for i, j, k in SECOND]


BONDS = (bond_list(0), bond_list(1))


def partner(o):
    return o if o < 8 else 8 + ((o - 8) ^ 1)


def row_shift(sub, target, dy):
    return dy + target - sub


def with_neighbours(atoms):
    result = set(atoms)
    for sub, x, y, z in atoms:
        for target, dx, dy, dz in BONDS[sub]:
            result.add((target, x + dx, y + dy, z + dz))
    return result


def columns_of(atoms):
    return sorted({atom[:3] for atom in atoms})


MAIN = columns_of(with_neighbours([(s, x, 0, 0) for s in (0, 1) for x in (0, 1)]))
LOW_SEED = [(1, x, -2, 63) for x in (0, 1)]
HIGH_SEED = [(0, x, 2, 0) for x in (0, 1)]
LOW_SIDE = [c for c in columns_of(with_neighbours(LOW_SEED)) if c not in MAIN]
HIGH_SIDE = [c for c in columns_of(with_neighbours(HIGH_SEED)) if c not in MAIN]
OWN = [(s, x, y, 0) for s in (0, 1) for x in range(4) for y in (0, 1)]
FINAL = columns_of(with_neighbours(OWN))


def places_of(atoms):
    return {(a[1], a[2]) for a in with_neighbours(with_neighbours(atoms))}


def phase_reads(h, y0):
    seeds = [(s, x, 0, z) for s in (0, 1) for x in (0, 1) for z in (0, 64)]
    places = places_of(seeds + LOW_SEED + HIGH_SEED)
    return {(x + 2 * h, y + y0) for x, y in places}


FINAL_READS = places_of(OWN)


def message_places(h, y0, dgx, e):
    return {(4 * dgx + 2 * h + x, y0 + 2 * e) for x in (0, 1)}


def sources(h, y0):
    later = [(h, y0, phase_reads(h, y0)) for h, y0 in PHASES[2 * h + y0 + 1 :]]
    later.append((2, 0, FINAL_READS))
    result = {}
    for dgx in (0, 1, -1):
        for e in (0, 1, -1, 2, -2):
            if (dgx, e) == (0, 0):
                continue
            for rank, (_, _, reads) in enumerate(later):
                if message_places(h, y0, dgx, e) & reads:
                    result[(dgx, e)] = 2 * h + y0 + 1 + rank
                    break
    return result


PHASES = [(0, 0), (0, 1), (1, 0), (1, 1)]
SOURCES = [sources(h, y0) for h, y0 in PHASES]
ORDERED = [sorted(found, key=lambda d: (found[d], d)) for found in SOURCES]


def sine_cosine(x):
    n = jnp.floor(x * (2.0 / math.pi) + 0.5)
    y = ((x - n * 1.5703125) - n * 4.83751296997e-4) - n * 7.54978995489e-8
    y2 = y * y
    sine = y + y * y2 * (-1.6666654611e-1 + y2 * (8.3321608736e-3 - y2 * 1.9515295891e-4))
    cosine = 1.0 - 0.5 * y2 + y2 * y2 * (
        4.166664568298827e-2 + y2 * (-1.388731625493765e-3 + y2 * 2.443315711809948e-5)
    )
    quarter = n - 4.0 * jnp.floor(0.25 * n)
    odd = (quarter == 1.0) | (quarter == 3.0)
    first, second = jnp.where(odd, cosine, sine), jnp.where(odd, sine, cosine)
    first = jnp.where(quarter >= 2.0, -first, first)
    second = jnp.where((quarter == 1.0) | (quarter == 2.0), -second, second)
    return first, second


def exchange(rows):
    shape = rows[0].shape
    place = lax.broadcasted_iota(jnp.int32, shape, 1)
    rows = list(rows)
    for step in (4, 2, 1):
        low = (place & step) == 0
        for i in range(8):
            if i & step:
                continue
            a, b = rows[i], rows[i + step]
            rows[i] = jnp.where(low, a, pltpu.roll(b, step, 1))
            rows[i + step] = jnp.where(low, pltpu.roll(a, 8 - step, 1), b)
    return rows


def rolled(value, dz):
    return value if dz == 0 else pltpu.roll(value, (-dz) % 128, value.ndim - 1)


def kernel(
    n_gx,
    n_yz,
    spin_hbm,
    pair_hbm,
    mix_hbm,
    bias_hbm,
    out_w_hbm,
    both_out,
    state,
    cosine,
    slope,
    by_bond,
    first_w,
    second_w,
    scratch_w,
    spin_ref,
    pair_ref,
    mix_ref,
    bias_ref,
    out_w_ref,
    load_sem,
    start_yz,
    start_gx,
    send_buf,
    got,
    start_send,
    start_recv,
    send_sem,
    recv_sem,
):
    gx = lax.axis_index("gx")
    yz = lax.axis_index("yz")

    def device(dgx, dyz):
        return (lax.rem(gx + dgx + n_gx, n_gx), lax.rem(yz + dyz + n_yz, n_yz))

    barrier = pltpu.get_barrier_semaphore()
    partners = [(0, d) for d in DELTAS] + [(s, d) for s in (1, -1) for d in GX_DELTAS]
    for dgx, dyz in partners:
        pl.semaphore_signal(barrier, inc=1, device_id=device(dgx, dyz), device_id_type=MESH)

    loads = []
    for j, (source, target) in enumerate(
        (
            (spin_hbm, spin_ref),
            (pair_hbm, pair_ref),
            (mix_hbm, mix_ref),
            (bias_hbm, bias_ref),
            (out_w_hbm, out_w_ref),
        )
    ):
        load = pltpu.make_async_copy(source, target, load_sem.at[j])
        load.start()
        loads.append(load)
    slope[...] = jnp.zeros(slope.shape, F32)
    state[...] = jnp.zeros(state.shape, F32)

    pl.semaphore_wait(barrier, len(partners))

    starts = []
    for j, d in enumerate(DELTAS):
        starts.append(
            pltpu.make_async_remote_copy(
                src_ref=spin_hbm,
                dst_ref=start_yz.at[j],
                send_sem=start_send.at[j],
                recv_sem=start_recv.at[j],
                device_id=device(0, d),
                device_id_type=MESH,
            )
        )
    for j, d in enumerate(GX_DELTAS):
        starts.append(
            pltpu.make_async_remote_copy(
                src_ref=spin_hbm.at[:, :, (3 if abs(d) == 2 else 2) : 4],
                dst_ref=start_gx.at[j, :, :, (1 if abs(d) == 2 else 0) : 2],
                send_sem=start_send.at[4 + j],
                recv_sem=start_recv.at[4 + j],
                device_id=device(1, d),
                device_id_type=MESH,
            )
        )
    for copy in starts[:3:-1] + starts[:4]:
        copy.start()

    for load in loads:
        load.wait()
    scratch_w[...] = jnp.zeros((128, 128), F32)
    for k in range(NB):
        scratch_w[16 * k : 16 * k + 8, :] = pair_ref[pl.ds(k, 8, stride=8), :]
        scratch_w[16 * k + 8 : 16 * k + 14, :] = pair_ref[pl.ds(64 + k, 6, stride=8), :]
    merged = jnp.dot(
        scratch_w[...],
        mix_ref[...],
        precision=lax.Precision.HIGHEST,
        preferred_element_type=F32,
    )
    row = lax.broadcasted_iota(jnp.int32, (128, 128), 0)
    with_bias = jnp.where(row == 14, jnp.broadcast_to(bias_ref[...], (128, 128)), merged)
    degree = (row // 16 + 1).astype(F32)
    scaled = -merged * degree * jnp.broadcast_to(out_w_ref[...], (128, 128))

    def stacked(matrix):
        high = matrix.astype(BF16)
        low = (matrix - high.astype(F32)).astype(BF16)
        return jnp.concatenate(
            [jnp.concatenate([high, high], 1), jnp.concatenate([low, low], 1)], 0
        )

    first_w[...] = stacked(0.5 * with_bias.T)
    second_w[...] = stacked(scaled)
    def put(value_of_sub, first_x, count, y, rows):
        for sub in (0, 1):
            r = y + 4 + sub
            state[1, :, sub, first_x : first_x + count, r : r + rows, :] = value_of_sub(sub)

    def roll_all(first_x, count):
        for sub in (0, 1):
            value = state[1, :, sub, first_x : first_x + count]
            state[0, :, sub, first_x : first_x + count] = rolled(value, -1)
            state[2, :, sub, first_x : first_x + count] = rolled(value, 1)

    put(lambda sub: spin_ref[:, sub], 2, 4, 0, 2)
    for copy in starts:
        copy.wait()
    for j, d in enumerate(DELTAS):
        put(lambda sub: start_yz[j, :, sub], 2, 4, -2 * d, 2)
    for j, d in enumerate(GX_DELTAS):
        first = 1 if abs(d) == 2 else 0
        put(lambda sub: start_gx[j, :, sub, first:], first, 2 - first, -2 * d, 2)
    roll_all(0, 6)

    def cosines(first_x, y0, low, high):
        r0, count = 1 + y0, high - low
        for sub in (0, 1):
            centre = state[1, :, sub, first_x + low : first_x + high, r0 : r0 + 8]
            for half in (0, 1):
                values = []
                for target, dx, dy, dz in BONDS[sub][8 * half : 8 * half + 8]:
                    r, x = r0 + row_shift(sub, target, dy), first_x + low + dx
                    product = centre * state[1 + dz, :, target, x : x + count, r : r + 8]
                    values.append(product[0] + product[1] + product[2])
                values += [jnp.ones((count, 8, 128), F32)] * (8 - len(values))
                for slot, value in enumerate(exchange(values)):
                    if 1 <= slot <= 6:
                        cosine[half, sub, low:high, slot] = value

    def load_cosine(column):
        sub, x, y = column
        return jnp.concatenate([cosine[half, sub, x + 1, y + 3 + sub] for half in (0, 1)], 0)

    def store_slope(column, value):
        sub, x, y = column
        for half in (0, 1):
            slope[half, sub, x + 1, y + 3 + sub] = value[8 * half : 8 * half + 8, :]

    def slopes_by_bond(count):
        for sub in (0, 1):
            for half, low, high in ((0, 1 - sub, count - sub), (1, 1, count - 1)):
                zero = jnp.zeros((high - low, 8, 128), F32)
                values = [slope[half, sub, low:high, slot] for slot in range(1, 7)]
                for o, value in enumerate(exchange([zero] + values + [zero])):
                    if 8 * half + o < 14:
                        by_bond[sub, 8 * half + o, low:high, 8:16, :] = value
            for o, xi in ((0, 0), (1, count - 1)):
                for slot in range(1, 7):
                    by_bond[sub, 8 + o, xi, 8 + slot : 9 + slot, :] = slope[
                        1, sub, xi, slot, o : o + 1, :
                    ]

    def product(weight, value):
        high = value.astype(BF16)
        low = (value - high.astype(F32)).astype(BF16)
        wide = jnp.dot(
            weight[...], jnp.concatenate([high, low], 0), preferred_element_type=F32
        )
        return wide[:128] + wide[128:]

    def network(values):
        results = []
        for begin in range(0, len(values), CHUNK):
            part = values[begin : begin + CHUNK]
            c = jnp.concatenate(part, 1)
            twice = c + c
            firsts = [None, twice, twice * twice - 2.0]
            for _ in range(3, NB + 1):
                firsts.append(twice * firsts[-1] - firsts[-2])
            seconds = [None, twice, firsts[2] + 1.0]
            for k in range(3, NB):
                seconds.append(firsts[k] + seconds[k - 2])
            u = jnp.tanh(product(first_w, jnp.concatenate(firsts[1:], 0)))
            d = product(second_w, 1.0 - u * u)
            g = d[0:16]
            for k in range(1, NB):
                g = g + d[16 * k : 16 * k + 16] * seconds[k]
            results += [g[:, 128 * j : 128 * j + 128] for j in range(len(part))]
        return results

    lane = lax.broadcasted_iota(jnp.int32, (16, 128), 1)

    def packed(groups):
        result = None
        for first, columns in groups:
            order = (lane + (256 - first)) & 127
            for m, column in enumerate(columns):
                value = load_cosine(column)
                if m:
                    value = pltpu.roll(value, 4 * m, 1)
                if result is None:
                    result = value
                else:
                    inside = (order >= 4 * m) & (order < 4 * m + 4)
                    result = jnp.where(inside, value, result)
        return result

    def packed_pair(columns):
        result = None
        low = (lane + (256 - 63)) & 127
        high = (lane + (256 - 125)) & 127
        for m, column in enumerate(columns):
            value = load_cosine(column)
            if m:
                value = pltpu.roll(value, 4 * m, 1)
                inside = ((low >= 4 * m) & (low < 4 * m + 4)) | (
                    (high >= 4 * m) & (high < 4 * m + 4)
                )
                value = jnp.where(inside, value, result)
            result = value
        return result

    def spread(value, columns):
        for m, column in enumerate(columns):
            store_slope(column, pltpu.roll(value, 128 - 4 * m, 1) if m else value)

    def fields(sub, xi0, count, first_x, y0):
        r0 = 1 + y0
        total = None
        for o, (target, dx, dy, dz) in enumerate(BONDS[sub]):
            shift = row_shift(sub, target, dy)
            own = by_bond[sub, o, xi0 : xi0 + count, 8:16, :]
            r, xi = 8 + shift, xi0 + dx
            theirs = by_bond[target, partner(o), xi : xi + count, r : r + 8, :]
            coefficient = own + rolled(theirs, dz)
            spins = state[
                1 + dz,
                :,
                target,
                first_x + xi0 + dx : first_x + xi0 + dx + count,
                r0 + shift : r0 + shift + 8,
                :,
            ]
            term = coefficient[None] * spins
            total = term if total is None else total + term
        return total

    def rotate(spin, field):
        w = [TIME_STEP * field[c] for c in range(3)]
        s = [spin[c] for c in range(3)]
        square = w[0] * w[0] + w[1] * w[1] + w[2] * w[2]
        tiny = square < 1e-30
        size = jnp.sqrt(jnp.where(tiny, 1.0, square))
        sine, cosine_half = sine_cosine(0.5 * size)
        inverse = 1.0 / size
        half = jnp.where(tiny, 0.5, sine * inverse)
        ratio = 2.0 * half * jnp.where(tiny, 1.0, cosine_half)
        versine = 2.0 * half * half
        turn = 1.0 - versine * jnp.where(tiny, 0.0, square)
        along = versine * (w[0] * s[0] + w[1] * s[1] + w[2] * s[2])
        cross = [
            w[1] * s[2] - w[2] * s[1],
            w[2] * s[0] - w[0] * s[2],
            w[0] * s[1] - w[1] * s[0],
        ]
        return jnp.concatenate(
            [(turn * s[c] + ratio * cross[c] + along * w[c])[None] for c in range(3)], 0
        )

    shape = (3, 2, 8, 128)
    slot_of = lax.broadcasted_iota(jnp.int32, shape, 2)
    z_of = lax.broadcasted_iota(jnp.int32, shape, 3)
    seam = ((z_of >= 64) & (z_of < 66)) | (z_of >= 126)

    def write_targets(sub, first_x, y0, value):
        r0 = 1 + y0
        for dz in (-1, 0, 1):
            state[1 + dz, :, sub, first_x + 1 : first_x + 3, r0 : r0 + 8, :] = rolled(value, dz)

    def evaluate(columns):
        for column, value in zip(columns, network([load_cosine(c) for c in columns])):
            store_slope(column, value)

    def split(columns, arriving, origin):
        early, late = [], []
        for sub, x, y in columns:
            around = {(a[1] + origin[0], a[2] + origin[1]) for a in with_neighbours([(sub, x, y, 0)])}
            (late if around & arriving else early).append((sub, x, y))
        return early, late

    def gather(columns, first_x, y0, origin, reader):
        count = 4 if reader < 4 else NXI
        cosines_of = functools.partial(cosines, first_x, y0)
        if reader == 0:
            cosines_of(0, count)
            return columns
        for p in range(reader - 1):
            for source in ORDERED[p]:
                if SOURCES[p][source] == reader:
                    receive(p, source)
            reroll(p, reader, (0, 1, -1))
        p = reader - 1
        tiers = []
        late = [d for d in ORDERED[p] if SOURCES[p][d] == reader]
        if reader in (1, 3):
            parts = ([(0, 1)], [d for d in late if d != (0, 1)])
        else:
            parts = ([d for d in late if d[0] == 0], [d for d in late if d[0] != 0])
        for found in parts:
            places = set().union(*[message_places(*PHASES[p], *d) for d in found])
            tiers.append((found, places, {d[0] for d in found}))
        cosines_of(0, count)
        for step, (found, places, sides) in enumerate(tiers):
            ready, columns = split(columns, set().union(*[t[1] for t in tiers[step:]]), origin)
            evaluate(ready)
            for source in found:
                receive(p, source)
            reroll(p, reader, sides)
            touched = [x + 2 - first_x for x, _ in places]
            cosines_of(max(0, min(touched) - 1), min(count, max(touched) + 2))
        return columns

    def phase(h, y0):
        x0 = 2 * h
        first_x = x0 + 1
        r0 = 1 + y0
        late = gather(MAIN, first_x, y0, (x0, y0), 2 * h + y0)
        sides = packed([(62, LOW_SIDE), (126, HIGH_SIDE)])
        results = network([load_cosine(c) for c in late] + [sides])
        for column, value in zip(late, results):
            store_slope(column, value)
        spread(results[-1], LOW_SIDE)
        spread(results[-1], HIGH_SIDE)
        slopes_by_bond(4)
        old, trial = [], []
        for sub in (0, 1):
            spin = state[1, :, sub, first_x + 1 : first_x + 3, r0 : r0 + 8, :]
            old.append(spin)
            trial.append(rotate(spin, fields(sub, 1, 2, first_x, y0)))
        for sub in (0, 1):
            if sub == 0:
                extra = (slot_of == 5) & (z_of == 0)
            else:
                extra = (slot_of == 2) & (z_of == 63)
            change = ((slot_of == 3 + sub) & (z_of < 64)) | extra
            write_targets(sub, first_x, y0, jnp.where(change, trial[sub], old[sub]))
        cosines(first_x, y0, 0, 4)
        groups = (MAIN[:9], MAIN[9:])
        results = network([packed_pair(columns) for columns in groups])
        for columns, value in zip(groups, results):
            spread(value, columns)
        slopes_by_bond(4)
        final = []
        for sub in (0, 1):
            spin = state[1, :, sub, first_x + 1 : first_x + 3, r0 : r0 + 8, :]
            again = rotate(spin, fields(sub, 1, 2, first_x, y0))
            late = (slot_of == 3 + sub) & (z_of >= 64)
            final.append(jnp.where(late, jnp.where(seam, again, trial[sub]), spin))
        for sub in (0, 1):
            send_buf[2 * h + y0, :, sub, :, :, :] = final[sub][:, :, 3 + sub : 4 + sub, :]
        send(2 * h + y0)
        for sub in (0, 1):
            write_targets(sub, first_x, y0, final[sub])

    started = {}

    def send(p):
        for j, (dgx, e) in enumerate(ORDERED[p]):
            copy = pltpu.make_async_remote_copy(
                src_ref=send_buf.at[p],
                dst_ref=got.at[p, j],
                send_sem=send_sem.at[p, j],
                recv_sem=recv_sem.at[p, j],
                device_id=device(-dgx, -e),
                device_id_type=MESH,
            )
            copy.start()
            started[(p, (dgx, e))] = copy

    def receive(p, source):
        started[(p, source)].wait()
        h, y0 = PHASES[p]
        j = ORDERED[p].index(source)
        dgx, e = source
        put(lambda sub: got[p, j, :, sub], 4 * dgx + 2 * h + 2, 2, y0 + 2 * e, 1)

    def reroll(p, reader, sides):
        h, _ = PHASES[p]
        for dgx in sides:
            if any(d[0] == dgx and SOURCES[p][d] == reader for d in ORDERED[p]):
                roll_all(4 * dgx + 2 * h + 2, 2)

    for p in range(4):
        phase(*PHASES[p])

    for sub in (0, 1):
        both_out[0, :, sub] = state[1, :, sub, 2:6, 4 + sub : 6 + sub, :]
    evaluate(gather(FINAL, 1, 0, (0, 0), 4))
    slopes_by_bond(NXI)
    for sub in (0, 1):
        total = fields(sub, 1, 4, 1, 0)
        both_out[1, :, sub] = total[:, :, 3 + sub : 5 + sub, :]


def solution(mesh):
    n_gx, n_yz = mesh.shape["gx"], mesh.shape["yz"]

    def per_device(spin, pair, mix, bias, out_w):
        brick = jax.ShapeDtypeStruct(spin.shape, F32)
        vmem = pl.BlockSpec(memory_space=pltpu.VMEM)
        dma = pltpu.SemaphoreType.DMA
        both = pl.pallas_call(
            functools.partial(kernel, n_gx, n_yz),
            out_shape=jax.ShapeDtypeStruct((2,) + spin.shape, F32),
            in_specs=[pl.BlockSpec(memory_space=pl.ANY)] * 5,
            out_specs=vmem,
            scratch_shapes=[
                pltpu.VMEM((3, 3, 2, 8, 16, 128), F32),
                pltpu.VMEM((2, 2, NXI, 8, 8, 128), F32),
                pltpu.VMEM((2, 2, NXI, 8, 8, 128), F32),
                pltpu.VMEM((2, 14, NXI, 24, 128), F32),
                pltpu.VMEM((256, 256), BF16),
                pltpu.VMEM((256, 256), BF16),
                pltpu.VMEM((128, 128), F32),
                pltpu.VMEM(spin.shape, F32),
                pltpu.VMEM(pair.shape, F32),
                pltpu.VMEM(mix.shape, F32),
                pltpu.VMEM((1, 128), F32),
                pltpu.VMEM((1, 128), F32),
                dma((5,)),
                pltpu.VMEM((4, 3, 2, 4, 2, 128), F32),
                pltpu.VMEM((5, 3, 2, 2, 2, 128), F32),
                pltpu.VMEM((4, 3, 2, 2, 1, 128), F32),
                pltpu.VMEM((4, 9, 3, 2, 2, 1, 128), F32),
                dma((9,)),
                dma((9,)),
                dma((4, 9)),
                dma((4, 9)),
            ],
            compiler_params=pltpu.CompilerParams(collective_id=0, has_side_effects=True),
        )(spin, pair, mix, bias.reshape(1, 128), out_w.reshape(1, 128))
        return both[0], both[1]

    placed = (P(None, None, "gx", "yz", None), P(), P(), P(), P())
    return jax.shard_map(
        per_device,
        mesh=mesh,
        in_specs=placed,
        out_specs=(P(None, None, "gx", "yz", None), P(None, None, "gx", "yz", None)),
        check_vma=False,
    )
```

```python
import functools
import math

import jax
import jax.numpy as jnp
from jax import lax
from jax.experimental import pallas as pl
from jax.experimental.pallas import tpu as pltpu
from jax.sharding import PartitionSpec as P

MESH = pl.DeviceIdType.MESH
NB = 8
NXI = 6
TIME_STEP = 0.1
CHUNK = 20
F32 = jnp.float32
BF16 = jnp.bfloat16

FIRST = [(i, j, k) for i in (-1, 0) for j in (-1, 0) for k in (-1, 0)]
SECOND = [(1, 0, 0), (-1, 0, 0), (0, 1, 0), (0, -1, 0), (0, 0, 1), (0, 0, -1)]
DELTAS = (1, -1, 2, -2)
GX_DELTAS = (0, 1, -1, 2, -2)


def bond_list(sub):
    sign = 1 - 2 * sub
    result = [(1 - sub, sign * i, sign * j, sign * k) for i, j, k in FIRST]
    return result + [(sub, i, j, k) for i, j, k in SECOND]


BONDS = (bond_list(0), bond_list(1))


def partner(o):
    return o if o < 8 else 8 + ((o - 8) ^ 1)


def row_shift(sub, target, dy):
    return dy + target - sub


def with_neighbours(atoms):
    result = set(atoms)
    for sub, x, y, z in atoms:
        for target, dx, dy, dz in BONDS[sub]:
            result.add((target, x + dx, y + dy, z + dz))
    return result


def columns_of(atoms):
    return sorted({atom[:3] for atom in atoms})


MAIN = columns_of(with_neighbours([(s, x, 0, 0) for s in (0, 1) for x in (0, 1)]))
LOW_SEED = [(1, x, -2, 63) for x in (0, 1)]
HIGH_SEED = [(0, x, 2, 0) for x in (0, 1)]
LOW_SIDE = [c for c in columns_of(with_neighbours(LOW_SEED)) if c not in MAIN]
HIGH_SIDE = [c for c in columns_of(with_neighbours(HIGH_SEED)) if c not in MAIN]
OWN = [(s, x, y, 0) for s in (0, 1) for x in range(4) for y in (0, 1)]
FINAL = columns_of(with_neighbours(OWN))


def places_of(atoms):
    return {(a[1], a[2]) for a in with_neighbours(with_neighbours(atoms))}


def phase_reads(h, y0):
    seeds = [(s, x, 0, z) for s in (0, 1) for x in (0, 1) for z in (0, 64)]
    places = places_of(seeds + LOW_SEED + HIGH_SEED)
    return {(x + 2 * h, y + y0) for x, y in places}


FINAL_READS = places_of(OWN)


def message_places(h, y0, dgx, e):
    return {(4 * dgx + 2 * h + x, y0 + 2 * e) for x in (0, 1)}


def sources(h, y0):
    later = [(h, y0, phase_reads(h, y0)) for h, y0 in PHASES[2 * h + y0 + 1 :]]
    later.append((2, 0, FINAL_READS))
    result = {}
    for dgx in (0, 1, -1):
        for e in (0, 1, -1, 2, -2):
            if (dgx, e) == (0, 0):
                continue
            for rank, (_, _, reads) in enumerate(later):
                if message_places(h, y0, dgx, e) & reads:
                    result[(dgx, e)] = 2 * h + y0 + 1 + rank
                    break
    return result


PHASES = [(0, 0), (0, 1), (1, 0), (1, 1)]
SOURCES = [sources(h, y0) for h, y0 in PHASES]
ORDERED = [sorted(found, key=lambda d: (found[d], d)) for found in SOURCES]


def sine_cosine(x):
    n = jnp.floor(x * (2.0 / math.pi) + 0.5)
    y = ((x - n * 1.5703125) - n * 4.83751296997e-4) - n * 7.54978995489e-8
    y2 = y * y
    sine = y + y * y2 * (-1.6666654611e-1 + y2 * (8.3321608736e-3 - y2 * 1.9515295891e-4))
    cosine = 1.0 - 0.5 * y2 + y2 * y2 * (
        4.166664568298827e-2 + y2 * (-1.388731625493765e-3 + y2 * 2.443315711809948e-5)
    )
    quarter = n - 4.0 * jnp.floor(0.25 * n)
    odd = (quarter == 1.0) | (quarter == 3.0)
    first, second = jnp.where(odd, cosine, sine), jnp.where(odd, sine, cosine)
    first = jnp.where(quarter >= 2.0, -first, first)
    second = jnp.where((quarter == 1.0) | (quarter == 2.0), -second, second)
    return first, second


def exchange(rows):
    shape = rows[0].shape
    place = lax.broadcasted_iota(jnp.int32, shape, 1)
    rows = list(rows)
    for step in (4, 2, 1):
        low = (place & step) == 0
        for i in range(8):
            if i & step:
                continue
            a, b = rows[i], rows[i + step]
            rows[i] = jnp.where(low, a, pltpu.roll(b, step, 1))
            rows[i + step] = jnp.where(low, pltpu.roll(a, 8 - step, 1), b)
    return rows


def rolled(value, dz):
    return value if dz == 0 else pltpu.roll(value, (-dz) % 128, value.ndim - 1)


def kernel(
    n_gx,
    n_yz,
    spin_hbm,
    pair_hbm,
    mix_hbm,
    bias_hbm,
    out_w_hbm,
    both_out,
    state,
    cosine,
    slope,
    by_bond,
    first_w,
    second_w,
    scratch_w,
    spin_ref,
    pair_ref,
    mix_ref,
    bias_ref,
    out_w_ref,
    load_sem,
    start_yz,
    start_gx,
    send_buf,
    got,
    start_send,
    start_recv,
    send_sem,
    recv_sem,
):
    gx = lax.axis_index("gx")
    yz = lax.axis_index("yz")

    def device(dgx, dyz):
        return (lax.rem(gx + dgx + n_gx, n_gx), lax.rem(yz + dyz + n_yz, n_yz))

    barrier = pltpu.get_barrier_semaphore()
    partners = [(0, d) for d in DELTAS] + [(s, d) for s in (1, -1) for d in GX_DELTAS]
    for dgx, dyz in partners[::-1]:
        pl.semaphore_signal(barrier, inc=1, device_id=device(dgx, dyz), device_id_type=MESH)

    loads = []
    for j, (source, target) in enumerate(
        (
            (spin_hbm, spin_ref),
            (pair_hbm, pair_ref),
            (mix_hbm, mix_ref),
            (bias_hbm, bias_ref),
            (out_w_hbm, out_w_ref),
        )
    ):
        load = pltpu.make_async_copy(source, target, load_sem.at[j])
        load.start()
        loads.append(load)

    pl.semaphore_wait(barrier, len(partners))

    starts = []
    for j, d in enumerate(DELTAS):
        starts.append(
            pltpu.make_async_remote_copy(
                src_ref=spin_hbm,
                dst_ref=start_yz.at[j],
                send_sem=start_send.at[j],
                recv_sem=start_recv.at[j],
                device_id=device(0, d),
                device_id_type=MESH,
            )
        )
    for j, d in enumerate(GX_DELTAS):
        starts.append(
            pltpu.make_async_remote_copy(
                src_ref=spin_hbm.at[:, :, (3 if abs(d) == 2 else 2) : 4],
                dst_ref=start_gx.at[j, :, :, (1 if abs(d) == 2 else 0) : 2],
                send_sem=start_send.at[4 + j],
                recv_sem=start_recv.at[4 + j],
                device_id=device(1, d),
                device_id_type=MESH,
            )
        )
    for copy in starts[:3:-1] + starts[:4]:
        copy.start()
    slope[...] = jnp.zeros(slope.shape, F32)
    state[...] = jnp.zeros(state.shape, F32)

    for load in loads:
        load.wait()
    scratch_w[...] = jnp.zeros((128, 128), F32)
    for k in range(NB):
        scratch_w[16 * k : 16 * k + 8, :] = pair_ref[pl.ds(k, 8, stride=8), :]
        scratch_w[16 * k + 8 : 16 * k + 14, :] = pair_ref[pl.ds(64 + k, 6, stride=8), :]
    merged = jnp.dot(
        scratch_w[...],
        mix_ref[...],
        precision=lax.Precision.HIGHEST,
        preferred_element_type=F32,
    )
    row = lax.broadcasted_iota(jnp.int32, (128, 128), 0)
    with_bias = jnp.where(row == 14, jnp.broadcast_to(bias_ref[...], (128, 128)), merged)
    degree = (row // 16 + 1).astype(F32)
    scaled = -merged * degree * jnp.broadcast_to(out_w_ref[...], (128, 128))

    def stacked(matrix):
        high = matrix.astype(BF16)
        low = (matrix - high.astype(F32)).astype(BF16)
        return jnp.concatenate(
            [jnp.concatenate([high, high], 1), jnp.concatenate([low, low], 1)], 0
        )

    first_w[...] = stacked(0.5 * with_bias.T)
    second_w[...] = stacked(scaled)
    def put(value_of_sub, first_x, count, y, rows):
        for sub in (0, 1):
            r = y + 4 + sub
            state[1, :, sub, first_x : first_x + count, r : r + rows, :] = value_of_sub(sub)

    def roll_all(first_x, count):
        for sub in (0, 1):
            value = state[1, :, sub, first_x : first_x + count]
            state[0, :, sub, first_x : first_x + count] = rolled(value, -1)
            state[2, :, sub, first_x : first_x + count] = rolled(value, 1)

    put(lambda sub: spin_ref[:, sub], 2, 4, 0, 2)
    for copy in starts:
        copy.wait()
    for j, d in enumerate(DELTAS):
        put(lambda sub: start_yz[j, :, sub], 2, 4, -2 * d, 2)
    for j, d in enumerate(GX_DELTAS):
        first = 1 if abs(d) == 2 else 0
        put(lambda sub: start_gx[j, :, sub, first:], first, 2 - first, -2 * d, 2)
    roll_all(0, 6)

    def cosines(first_x, y0, low, high):
        r0, count = 1 + y0, high - low
        for sub in (0, 1):
            centre = state[1, :, sub, first_x + low : first_x + high, r0 : r0 + 8]
            for half in (0, 1):
                values = []
                for target, dx, dy, dz in BONDS[sub][8 * half : 8 * half + 8]:
                    r, x = r0 + row_shift(sub, target, dy), first_x + low + dx
                    product = centre * state[1 + dz, :, target, x : x + count, r : r + 8]
                    values.append(product[0] + product[1] + product[2])
                values += [jnp.ones((count, 8, 128), F32)] * (8 - len(values))
                for slot, value in enumerate(exchange(values)):
                    if 1 <= slot <= 6:
                        cosine[half, sub, low:high, slot] = value

    def load_cosine(column):
        sub, x, y = column
        return jnp.concatenate([cosine[half, sub, x + 1, y + 3 + sub] for half in (0, 1)], 0)

    def store_slope(column, value):
        sub, x, y = column
        for half in (0, 1):
            slope[half, sub, x + 1, y + 3 + sub] = value[8 * half : 8 * half + 8, :]

    def slopes_by_bond(count):
        for sub in (0, 1):
            for half, low, high in ((0, 1 - sub, count - sub), (1, 1, count - 1)):
                zero = jnp.zeros((high - low, 8, 128), F32)
                values = [slope[half, sub, low:high, slot] for slot in range(1, 7)]
                for o, value in enumerate(exchange([zero] + values + [zero])):
                    if 8 * half + o < 14:
                        by_bond[sub, 8 * half + o, low:high, 8:16, :] = value
            for o, xi in ((0, 0), (1, count - 1)):
                for slot in range(1, 7):
                    by_bond[sub, 8 + o, xi, 8 + slot : 9 + slot, :] = slope[
                        1, sub, xi, slot, o : o + 1, :
                    ]

    def product(weight, value):
        high = value.astype(BF16)
        low = (value - high.astype(F32)).astype(BF16)
        wide = jnp.dot(
            weight[...], jnp.concatenate([high, low], 0), preferred_element_type=F32
        )
        return wide[:128] + wide[128:]

    def network(values):
        results = []
        for begin in range(0, len(values), CHUNK):
            part = values[begin : begin + CHUNK]
            c = jnp.concatenate(part, 1)
            twice = c + c
            firsts = [None, twice, twice * twice - 2.0]
            for _ in range(3, NB + 1):
                firsts.append(twice * firsts[-1] - firsts[-2])
            seconds = [None, twice, firsts[2] + 1.0]
            for k in range(3, NB):
                seconds.append(firsts[k] + seconds[k - 2])
            u = jnp.tanh(product(first_w, jnp.concatenate(firsts[1:], 0)))
            d = product(second_w, 1.0 - u * u)
            g = d[0:16]
            for k in range(1, NB):
                g = g + d[16 * k : 16 * k + 16] * seconds[k]
            results += [g[:, 128 * j : 128 * j + 128] for j in range(len(part))]
        return results

    lane = lax.broadcasted_iota(jnp.int32, (16, 128), 1)

    def packed(groups):
        result = None
        for first, columns in groups:
            order = (lane + (256 - first)) & 127
            for m, column in enumerate(columns):
                value = load_cosine(column)
                if m:
                    value = pltpu.roll(value, 4 * m, 1)
                if result is None:
                    result = value
                else:
                    inside = (order >= 4 * m) & (order < 4 * m + 4)
                    result = jnp.where(inside, value, result)
        return result

    def packed_pair(columns):
        result = None
        low = (lane + (256 - 63)) & 127
        high = (lane + (256 - 125)) & 127
        for m, column in enumerate(columns):
            value = load_cosine(column)
            if m:
                value = pltpu.roll(value, 4 * m, 1)
                inside = ((low >= 4 * m) & (low < 4 * m + 4)) | (
                    (high >= 4 * m) & (high < 4 * m + 4)
                )
                value = jnp.where(inside, value, result)
            result = value
        return result

    def spread(value, columns):
        for m, column in enumerate(columns):
            store_slope(column, pltpu.roll(value, 128 - 4 * m, 1) if m else value)

    def fields(sub, xi0, count, first_x, y0):
        r0 = 1 + y0
        total = None
        for o, (target, dx, dy, dz) in enumerate(BONDS[sub]):
            shift = row_shift(sub, target, dy)
            own = by_bond[sub, o, xi0 : xi0 + count, 8:16, :]
            r, xi = 8 + shift, xi0 + dx
            theirs = by_bond[target, partner(o), xi : xi + count, r : r + 8, :]
            coefficient = own + rolled(theirs, dz)
            spins = state[
                1 + dz,
                :,
                target,
                first_x + xi0 + dx : first_x + xi0 + dx + count,
                r0 + shift : r0 + shift + 8,
                :,
            ]
            term = coefficient[None] * spins
            total = term if total is None else total + term
        return total

    def rotate(spin, field):
        w = [TIME_STEP * field[c] for c in range(3)]
        s = [spin[c] for c in range(3)]
        square = w[0] * w[0] + w[1] * w[1] + w[2] * w[2]
        tiny = square < 1e-30
        size = jnp.sqrt(jnp.where(tiny, 1.0, square))
        sine, cosine_half = sine_cosine(0.5 * size)
        inverse = 1.0 / size
        half = jnp.where(tiny, 0.5, sine * inverse)
        ratio = 2.0 * half * jnp.where(tiny, 1.0, cosine_half)
        versine = 2.0 * half * half
        turn = 1.0 - versine * jnp.where(tiny, 0.0, square)
        along = versine * (w[0] * s[0] + w[1] * s[1] + w[2] * s[2])
        cross = [
            w[1] * s[2] - w[2] * s[1],
            w[2] * s[0] - w[0] * s[2],
            w[0] * s[1] - w[1] * s[0],
        ]
        return jnp.concatenate(
            [(turn * s[c] + ratio * cross[c] + along * w[c])[None] for c in range(3)], 0
        )

    shape = (3, 2, 8, 128)
    slot_of = lax.broadcasted_iota(jnp.int32, shape, 2)
    z_of = lax.broadcasted_iota(jnp.int32, shape, 3)
    seam = ((z_of >= 64) & (z_of < 66)) | (z_of >= 126)

    def write_targets(sub, first_x, y0, value):
        r0 = 1 + y0
        for dz in (-1, 0, 1):
            state[1 + dz, :, sub, first_x + 1 : first_x + 3, r0 : r0 + 8, :] = rolled(value, dz)

    def evaluate(columns):
        for column, value in zip(columns, network([load_cosine(c) for c in columns])):
            store_slope(column, value)

    def split(columns, arriving, origin):
        early, late = [], []
        for sub, x, y in columns:
            around = {(a[1] + origin[0], a[2] + origin[1]) for a in with_neighbours([(sub, x, y, 0)])}
            (late if around & arriving else early).append((sub, x, y))
        return early, late

    def gather(columns, first_x, y0, origin, reader):
        count = 4 if reader < 4 else NXI
        cosines_of = functools.partial(cosines, first_x, y0)
        if reader == 0:
            cosines_of(0, count)
            return columns
        for p in range(reader - 1):
            for source in ORDERED[p]:
                if SOURCES[p][source] == reader:
                    receive(p, source)
            reroll(p, reader, (0, 1, -1))
        p = reader - 1
        tiers = []
        late = [d for d in ORDERED[p] if SOURCES[p][d] == reader]
        if reader in (1, 3):
            parts = ([(0, 1)], [d for d in late if d != (0, 1)])
        else:
            parts = ([d for d in late if d[0] == 0], [d for d in late if d[0] != 0])
        for found in parts:
            places = set().union(*[message_places(*PHASES[p], *d) for d in found])
            tiers.append((found, places, {d[0] for d in found}))
        cosines_of(0, count)
        for step, (found, places, sides) in enumerate(tiers):
            ready, columns = split(columns, set().union(*[t[1] for t in tiers[step:]]), origin)
            evaluate(ready)
            for source in found:
                receive(p, source)
            reroll(p, reader, sides)
            touched = [x + 2 - first_x for x, _ in places]
            cosines_of(max(0, min(touched) - 1), min(count, max(touched) + 2))
        return columns

    def phase(h, y0):
        x0 = 2 * h
        first_x = x0 + 1
        r0 = 1 + y0
        late = gather(MAIN, first_x, y0, (x0, y0), 2 * h + y0)
        sides = packed([(62, LOW_SIDE), (126, HIGH_SIDE)])
        results = network([load_cosine(c) for c in late] + [sides])
        for column, value in zip(late, results):
            store_slope(column, value)
        spread(results[-1], LOW_SIDE)
        spread(results[-1], HIGH_SIDE)
        slopes_by_bond(4)
        old, trial = [], []
        for sub in (0, 1):
            spin = state[1, :, sub, first_x + 1 : first_x + 3, r0 : r0 + 8, :]
            old.append(spin)
            trial.append(rotate(spin, fields(sub, 1, 2, first_x, y0)))
        for sub in (0, 1):
            if sub == 0:
                extra = (slot_of == 5) & (z_of == 0)
            else:
                extra = (slot_of == 2) & (z_of == 63)
            change = ((slot_of == 3 + sub) & (z_of < 64)) | extra
            write_targets(sub, first_x, y0, jnp.where(change, trial[sub], old[sub]))
        cosines(first_x, y0, 0, 4)
        groups = (MAIN[:9], MAIN[9:])
        results = network([packed_pair(columns) for columns in groups])
        for columns, value in zip(groups, results):
            spread(value, columns)
        slopes_by_bond(4)
        final = []
        for sub in (0, 1):
            spin = state[1, :, sub, first_x + 1 : first_x + 3, r0 : r0 + 8, :]
            again = rotate(spin, fields(sub, 1, 2, first_x, y0))
            late = (slot_of == 3 + sub) & (z_of >= 64)
            final.append(jnp.where(late, jnp.where(seam, again, trial[sub]), spin))
        for sub in (0, 1):
            send_buf[2 * h + y0, :, sub, :, :, :] = final[sub][:, :, 3 + sub : 4 + sub, :]
        send(2 * h + y0)
        for sub in (0, 1):
            write_targets(sub, first_x, y0, final[sub])

    started = {}

    def send(p):
        for j, (dgx, e) in enumerate(ORDERED[p]):
            copy = pltpu.make_async_remote_copy(
                src_ref=send_buf.at[p],
                dst_ref=got.at[p, j],
                send_sem=send_sem.at[p, j],
                recv_sem=recv_sem.at[p, j],
                device_id=device(-dgx, -e),
                device_id_type=MESH,
            )
            copy.start()
            started[(p, (dgx, e))] = copy

    def receive(p, source):
        started[(p, source)].wait()
        h, y0 = PHASES[p]
        j = ORDERED[p].index(source)
        dgx, e = source
        put(lambda sub: got[p, j, :, sub], 4 * dgx + 2 * h + 2, 2, y0 + 2 * e, 1)

    def reroll(p, reader, sides):
        h, _ = PHASES[p]
        for dgx in sides:
            if any(d[0] == dgx and SOURCES[p][d] == reader for d in ORDERED[p]):
                roll_all(4 * dgx + 2 * h + 2, 2)

    for p in range(4):
        phase(*PHASES[p])

    for sub in (0, 1):
        both_out[0, :, sub] = state[1, :, sub, 2:6, 4 + sub : 6 + sub, :]
    evaluate(gather(FINAL, 1, 0, (0, 0), 4))
    slopes_by_bond(NXI)
    for sub in (0, 1):
        total = fields(sub, 1, 4, 1, 0)
        both_out[1, :, sub] = total[:, :, 3 + sub : 5 + sub, :]


def solution(mesh):
    n_gx, n_yz = mesh.shape["gx"], mesh.shape["yz"]

    def per_device(spin, pair, mix, bias, out_w):
        brick = jax.ShapeDtypeStruct(spin.shape, F32)
        vmem = pl.BlockSpec(memory_space=pltpu.VMEM)
        dma = pltpu.SemaphoreType.DMA
        both = pl.pallas_call(
            functools.partial(kernel, n_gx, n_yz),
            out_shape=jax.ShapeDtypeStruct((2,) + spin.shape, F32),
            in_specs=[pl.BlockSpec(memory_space=pl.ANY)] * 5,
            out_specs=vmem,
            scratch_shapes=[
                pltpu.VMEM((3, 3, 2, 8, 16, 128), F32),
                pltpu.VMEM((2, 2, NXI, 8, 8, 128), F32),
                pltpu.VMEM((2, 2, NXI, 8, 8, 128), F32),
                pltpu.VMEM((2, 14, NXI, 24, 128), F32),
                pltpu.VMEM((256, 256), BF16),
                pltpu.VMEM((256, 256), BF16),
                pltpu.VMEM((128, 128), F32),
                pltpu.VMEM(spin.shape, F32),
                pltpu.VMEM(pair.shape, F32),
                pltpu.VMEM(mix.shape, F32),
                pltpu.VMEM((1, 128), F32),
                pltpu.VMEM((1, 128), F32),
                dma((5,)),
                pltpu.VMEM((4, 3, 2, 4, 2, 128), F32),
                pltpu.VMEM((5, 3, 2, 2, 2, 128), F32),
                pltpu.VMEM((4, 3, 2, 2, 1, 128), F32),
                pltpu.VMEM((4, 9, 3, 2, 2, 1, 128), F32),
                dma((9,)),
                dma((9,)),
                dma((4, 9)),
                dma((4, 9)),
            ],
            compiler_params=pltpu.CompilerParams(collective_id=0, has_side_effects=True),
        )(spin, pair, mix, bias.reshape(1, 128), out_w.reshape(1, 128))
        return both[0], both[1]

    placed = (P(None, None, "gx", "yz", None), P(), P(), P(), P())
    return jax.shard_map(
        per_device,
        mesh=mesh,
        in_specs=placed,
        out_specs=(P(None, None, "gx", "yz", None), P(None, None, "gx", "yz", None)),
        check_vma=False,
    )
```
